512 devices in a mesh: ctx: 16 (over y_hi, x), set: 32 (over z, y_lo, core).
Axes of the slice: x: 4, y: 8 (y_hi: 4, y_lo: 2; y = y_hi * 2 + y_lo), z: 8, core: 2. Of those that a mesh axis runs over, the one named last changes fastest.
Arguments:
- queries: bfloat16 [32, 256, 2048], P('set', 'ctx'), may hold values from -160 to 160
- out_grad: bfloat16 [32, 256, 2048], P('set', 'ctx'), may hold values from -24 to 24
- branch_kv: bfloat16 [32, 256, 256], P('set', 'ctx'), may hold values from -10.75 to 10.75
- trunk_kv: bfloat16 [8192, 256], P('ctx'), may hold values from -6 to 6
- parent: int32 [32, 256], P('set'), may hold values from -1 to 254, as said below
- prefix: int32 [32, 256], P('set'), may hold values from 2048 to 8192, as said below
Outputs:
- query_grad: bfloat16 [32, 256, 2048], P('set', 'ctx')
- branch_grad: float32 [32, 256, 256], P('set', 'ctx')
- trunk_grad: float32 [8192, 256], P(('ctx', 'set'))
The draws below stay inside these ranges and needn't reach their ends.
Inputs may be any that keep to these rules, and one draw needn't show every extreme that they name: parent[s, r] is -1 for r a multiple of 64, else between max(r - 32, 0) and r - 1; the last row's parent is row 254. `prefix`: row 0 of every set sees the whole trunk.
All inputs are finite; a program needn't handle non-finite values.
Results may differ from the reference program's by a relative error of at most 0.005.
Values may be sent and summed in bfloat16 or wider, within the bound.
No kernel may reach another device: no remote copies, remote signals or barrier semaphores. Data moves between devices by JAX's collectives and lax.ppermute only.
A program may use at most 64 MiB of HBM per device.

```python
import jax
import jax.numpy as jnp
from jax import lax

HEADS = 16
HD = 128
R = 256
SETS = 32
TRUNK = 8192


def anchor_key(key):
    flips = jax.random.bernoulli(jax.random.fold_in(key, 23), 0.5, (HD,))
    return jnp.where(flips, 4.0, -4.0).astype(jnp.float32)


def trunk_values(key):
    noise = jax.random.truncated_normal(jax.random.fold_in(key, 7), -6.0, 6.0, (TRUNK, 2 * HD), jnp.float32)
    anchor = anchor_key(key)
    lowered = jnp.arange(HD, dtype=jnp.int32) < max(HD // 8, 1)
    second = jnp.where(lowered, anchor * 0.9375, anchor)
    noise = noise.at[TRUNK - 1, :HD].set(anchor)
    noise = noise.at[TRUNK - 2, :HD].set(second)
    return noise


def draw_trunk_kv(key, part):
    return trunk_values(key).astype(jnp.bfloat16)


def draw_queries(key, part):
    base = 2.0 * jax.random.truncated_normal(jax.random.fold_in(key, 11), -6.0, 6.0, (SETS, R, HEADS * HD), jnp.float32)
    anchor = anchor_key(key)
    target = 150.0 + 250.0 * jnp.arange(HEADS, dtype=jnp.float32) / max(HEADS - 1, 1)
    strength = target / (16.0 * HD ** 0.5)
    aligned = (strength[:, None] * anchor[None, :]).reshape(HEADS * HD)
    base = base.at[:, 0, :].set(jnp.broadcast_to(aligned[None, :], (SETS, HEADS * HD)))
    return base.astype(jnp.bfloat16)


def draw_parent(key, part):
    labels = jnp.arange(R, dtype=jnp.int32)
    lowest = jnp.maximum(labels - 32, 0)
    picks = jax.random.randint(jax.random.fold_in(key, 13), (SETS, R), 0, 1 << 20, dtype=jnp.int32)
    spread = jnp.maximum(labels - lowest, 1)
    linked = lowest[None, :] + picks % spread[None, :]
    linked = jnp.where(labels[None, :] == R - 1, R - 2, linked)
    return jnp.where(labels[None, :] % 64 == 0, -1, linked).astype(jnp.int32)


def draw_prefix(key, part):
    lengths = jax.random.randint(jax.random.fold_in(key, 17), (SETS, R), TRUNK // 4, TRUNK + 1, dtype=jnp.int32)
    labels = jnp.arange(R, dtype=jnp.int32)
    return jnp.where(labels[None, :] == 0, TRUNK, lengths).astype(jnp.int32)


def level_of(rng, extent, split, least, largest):
    def one(position, shards_of):
        heights = jax.random.uniform(jax.random.fold_in(jax.random.fold_in(rng, 6), position), (shards_of,), jnp.float32, least / len(split), largest / len(split))
        return jnp.repeat(jnp.exp(heights), extent[position] // shards_of).reshape((-1,) + (1,) * (len(extent) - position - 1))

    loudness = one(*split[0])
    for cut in split[1:]:
        loudness = loudness * one(*cut)
    return loudness


def scatter_about(stream_key, dims, scale, limit, pieces=(), held_as=jnp.bfloat16):
    array = jax.random.normal(stream_key, dims, jnp.float32) * scale
    if len(pieces) > 0:
        array = level_of(stream_key, dims, pieces, -0.22, 0.18) * array
    return jnp.clip(array, min=-limit, max=limit).astype(held_as)


def setup_inputs(seed: int = 0) -> dict:
    streams_of = jax.random.split(jax.random.key(seed), 7)
    queries = draw_queries(jax.random.fold_in(streams_of[6], 71), 0)
    out_grad = scatter_about(streams_of[1], (SETS, R, HEADS * HD), 4.0, 24.0, ((0, 32), (1, 16)))
    branch_kv = scatter_about(streams_of[2], (SETS, R, 2 * HD), 1.8, 10.75, ((0, 32), (1, 16)))
    trunk_kv = draw_trunk_kv(jax.random.fold_in(streams_of[6], 71), 0)
    parent = draw_parent(jax.random.fold_in(streams_of[6], 71), 0)
    prefix = draw_prefix(jax.random.fold_in(streams_of[6], 71), 0)
    return {"queries": queries, "out_grad": out_grad, "branch_kv": branch_kv, "trunk_kv": trunk_kv, "parent": parent, "prefix": prefix}


MASKED = -1.0e30


def ancestors(parent_row):
    count = parent_row.shape[0]
    labels = jnp.arange(count, dtype=jnp.int32)
    links = (parent_row[:, None] == labels[None, :]) | (labels[:, None] == labels[None, :])
    reach = links.astype(jnp.bfloat16)
    for level in range(max(count - 1, 1).bit_length()):
        reach = jnp.minimum(jnp.dot(reach, reach, preferred_element_type=jnp.float32), 1.0).astype(jnp.bfloat16)
    return reach > 0.5


def reference(queries, out_grad, branch_kv, trunk_kv, parent, prefix):
    width = HD
    scale = HD ** -0.5
    keys = trunk_kv[:, :width]
    values = trunk_kv[:, width:]
    key_ids = jnp.arange(TRUNK, dtype=jnp.int32)

    def one_set(kv_grad, inputs):
        query_set, grad_set, branch_set, parent_row, prefix_row = inputs
        reach = ancestors(parent_row)
        trunk_mask = key_ids[None, :] < prefix_row[:, None]
        branch_keys = branch_set[:, :width]
        branch_values = branch_set[:, width:]
        query_heads = query_set.reshape(R, HEADS, width).transpose(1, 0, 2)
        grad_heads = grad_set.reshape(R, HEADS, width).transpose(1, 0, 2)

        def one_head(carry, pair):
            kv_acc, branch_acc = carry
            query_head, grad_head = pair
            trunk_scores = jnp.where(trunk_mask, scale * jnp.dot(query_head, keys.T, preferred_element_type=jnp.float32), MASKED)
            branch_scores = jnp.where(reach, scale * jnp.dot(query_head, branch_keys.T, preferred_element_type=jnp.float32), MASKED)
            top = jnp.maximum(jnp.max(trunk_scores, axis=1), jnp.max(branch_scores, axis=1))
            total = jnp.sum(jnp.where(trunk_mask, jnp.exp(trunk_scores - top[:, None]), 0.0), axis=1)
            total = total + jnp.sum(jnp.where(reach, jnp.exp(branch_scores - top[:, None]), 0.0), axis=1)
            log_total = top + jnp.log(total)
            trunk_probs = jnp.where(trunk_mask, jnp.exp(trunk_scores - log_total[:, None]), 0.0)
            branch_probs = jnp.where(reach, jnp.exp(branch_scores - log_total[:, None]), 0.0)
            trunk_slopes = jnp.dot(grad_head, values.T, preferred_element_type=jnp.float32)
            branch_slopes = jnp.dot(grad_head, branch_values.T, preferred_element_type=jnp.float32)
            delta = jnp.sum(trunk_probs * trunk_slopes, axis=1) + jnp.sum(branch_probs * branch_slopes, axis=1)
            trunk_dscore = (trunk_probs * (trunk_slopes - delta[:, None])).astype(jnp.bfloat16)
            branch_dscore = (branch_probs * (branch_slopes - delta[:, None])).astype(jnp.bfloat16)
            query_grad = scale * jnp.dot(trunk_dscore, keys, preferred_element_type=jnp.float32)
            query_grad = query_grad + scale * jnp.dot(branch_dscore, branch_keys, preferred_element_type=jnp.float32)
            trunk_probs_low = trunk_probs.astype(jnp.bfloat16)
            trunk_k = scale * jnp.dot(trunk_dscore.T, query_head, preferred_element_type=jnp.float32)
            trunk_v = jnp.dot(trunk_probs_low.T, grad_head, preferred_element_type=jnp.float32)
            kv_acc = kv_acc + jnp.concatenate([trunk_k, trunk_v], axis=1)
            branch_probs_low = branch_probs.astype(jnp.bfloat16)
            branch_k = scale * jnp.dot(branch_dscore.T, query_head, preferred_element_type=jnp.float32)
            branch_v = jnp.dot(branch_probs_low.T, grad_head, preferred_element_type=jnp.float32)
            branch_acc = branch_acc + jnp.concatenate([branch_k, branch_v], axis=1)
            return (kv_acc, branch_acc), query_grad

        branch_init = jnp.zeros((R, 2 * width), jnp.float32)
        (kv_grad, branch_grad), head_grads = lax.scan(one_head, (kv_grad, branch_init), (query_heads, grad_heads))
        query_grad = head_grads.transpose(1, 0, 2).reshape(R, HEADS * width).astype(jnp.bfloat16)
        return kv_grad, (query_grad, branch_grad)

    kv_init = jnp.zeros((TRUNK, 2 * width), jnp.float32)
    kv_grad, (query_grads, branch_grads) = lax.scan(one_set, kv_init, (queries, out_grad, branch_kv, parent, prefix))
    return query_grads, branch_grads, kv_grad
```

```python
import jax
import jax.numpy as jnp
from jax import lax
from jax.experimental import pallas as pl
from jax.experimental.pallas import tpu as pltpu
from jax.sharding import Mesh, PartitionSpec as P

MASKED = -1e30
TILE = 16
SET = ("z", "yl", "c")


def ancestors_t(parent_row):
    count = parent_row.shape[0]
    labels = jnp.arange(count, dtype=jnp.int32)
    links = (parent_row[None, :] == labels[:, None]) | (labels[:, None] == labels[None, :])
    reach = links.astype(jnp.bfloat16)
    for level in range(max(count - 1, 1).bit_length()):
        reach = jnp.minimum(jnp.dot(reach, reach, preferred_element_type=jnp.float32), 1.0).astype(
            jnp.bfloat16
        )
    return reach


def dot_nt(left, right):
    return lax.dot_general(
        left, right, (((1,), (1,)), ((), ())), preferred_element_type=jnp.float32
    )


def dot_tn(left, right):
    return lax.dot_general(
        left, right, (((0,), (0,)), ((), ())), preferred_element_type=jnp.float32
    )


def stack_heads(src, dst):
    groups, own, _ = src.shape
    width = dst.shape[1]
    rows = groups * own
    for h in range(dst.shape[0] // rows):
        for y in range(groups):
            dst[pl.ds(h * rows + y * own, own), :] = src[y, :, pl.ds(h * width, width)]


def stats_kernel(lim_ref, reach_ref, q_ref, g_ref, kv_ref, out_ref, qs, gs, s_scr, g_scr):
    blocks, keys, wide = kv_ref.shape
    width = wide // 2
    lanes = qs.shape[0]
    scale = width ** (-0.5)
    trunk = keys - TILE
    stack_heads(q_ref, qs)
    stack_heads(g_ref, gs)
    ids = lax.broadcasted_iota(jnp.int32, (TILE, lanes), 0)
    room = jnp.broadcast_to(lim_ref[...], (TILE, lanes)) - ids

    def block(b, carry):
        top, total, slope = carry
        s_scr[...] = dot_nt(kv_ref[b, :, :width], qs[...])
        g_scr[...] = dot_nt(kv_ref[b, :, width:], gs[...])

        def mask(t, best):
            at = pl.ds(t * TILE, TILE)
            s = jnp.where(room > b * trunk + t * TILE, s_scr[at, :] * scale, MASKED)
            s_scr[at, :] = s
            return jnp.maximum(best, s)

        best = lax.fori_loop(0, trunk // TILE, mask, jnp.full((TILE, lanes), MASKED, jnp.float32), unroll=2)
        tree = jnp.where(
            reach_ref[pl.ds(b * TILE, TILE), :] > 0.5, s_scr[trunk:, :] * scale, MASKED
        )
        s_scr[trunk:, :] = tree
        best = jnp.max(jnp.maximum(best, tree), axis=0, keepdims=True)
        now = jnp.maximum(top, best)
        fade = jnp.exp(top - now)

        def add(t, sums):
            at = pl.ds(t * TILE, TILE)
            p = jnp.exp(s_scr[at, :] - now)
            return (sums[0] + p, sums[1] + p * g_scr[at, :])

        zero = jnp.zeros((TILE, lanes), jnp.float32)
        l, d = lax.fori_loop(0, keys // TILE, add, (zero, zero), unroll=3)
        return (
            now,
            total * fade + jnp.sum(l, axis=0, keepdims=True),
            slope * fade + jnp.sum(d, axis=0, keepdims=True),
        )

    zero = jnp.zeros((1, lanes), jnp.float32)
    top, total, slope = lax.fori_loop(0, blocks, block, (zero + MASKED, zero, zero))
    out_ref[0:1, :] = top + jnp.log(total)
    out_ref[1:2, :] = slope / total


def grads_kernel(
    core_ref, lim_ref, reach_ref, stats_ref, q_ref, g_ref, kv_ref,
    dq_ref, keep_ref, send_ref, tree_ref,
    qs, gs, s_scr, g_scr, d_scr, p_scr, kv_scr, dq_scr,
):
    blocks, keys, wide = kv_ref.shape
    width = wide // 2
    lanes = qs.shape[0]
    scale = width ** (-0.5)
    trunk = keys - TILE
    groups = q_ref.shape[0]
    rows = groups * q_ref.shape[1]
    mine = core_ref[0]
    stack_heads(q_ref, qs)
    stack_heads(g_ref, gs)
    parts = [stats_ref[i, 0:1, :] for i in range(groups)]
    top = parts[0]
    for part in parts[1:]:
        top = jnp.maximum(top, part)
    weights = [jnp.exp(part - top) for part in parts]
    total = weights[0]
    for weight in weights[1:]:
        total = total + weight
    log_total = top + jnp.log(total)
    delta = jnp.zeros_like(top)
    for i in range(groups):
        delta = delta + jnp.exp(parts[i] - log_total) * stats_ref[i, 1:2, :]
    ids = lax.broadcasted_iota(jnp.int32, (TILE, lanes), 0)
    room = jnp.broadcast_to(lim_ref[...], (TILE, lanes)) - ids
    dq_scr[...] = jnp.zeros_like(dq_scr)

    def finish(at, s):
        p = jnp.exp(s - log_total)
        d_scr[at, :] = (p * (g_scr[at, :] - delta)).astype(jnp.bfloat16)
        p_scr[at, :] = p.astype(jnp.bfloat16)

    @pl.loop(0, blocks)
    def _(b):
        k = kv_ref[b, :, :width]
        s_scr[...] = dot_nt(k, qs[...])
        g_scr[...] = dot_nt(kv_ref[b, :, width:], gs[...])

        def tile(t, carry):
            at = pl.ds(pl.multiple_of(t * TILE, TILE), TILE)
            finish(at, jnp.where(room > b * trunk + t * TILE, s_scr[at, :] * scale, MASKED))
            return carry

        lax.fori_loop(0, trunk // TILE, tile, 0, unroll=2)
        finish(
            pl.ds(trunk, TILE),
            jnp.where(reach_ref[pl.ds(b * TILE, TILE), :] > 0.5, s_scr[trunk:, :] * scale, MASKED),
        )
        dk = scale * jnp.dot(d_scr[...], qs[...], preferred_element_type=jnp.float32)
        dv = jnp.dot(p_scr[...], gs[...], preferred_element_type=jnp.float32)
        kv_scr[:, :, :, :width] = dk[:trunk].reshape(trunk // (2 * TILE), 2, TILE, width)
        kv_scr[:, :, :, width:] = dv[:trunk].reshape(trunk // (2 * TILE), 2, TILE, width)
        tree_ref[b, :, :width] = dk[trunk:]
        tree_ref[b, :, width:] = dv[trunk:]
        keep_ref[b] = kv_scr[:, mine]
        send_ref[b] = kv_scr[:, 1 - mine].astype(jnp.bfloat16)
        dq_scr[...] += dot_tn(k, d_scr[...])

    for h in range(lanes // rows):
        piece = (scale * dq_scr[:, pl.ds(h * rows, rows)]).T
        dq_ref[:, :, pl.ds(h * width, width)] = piece.reshape(groups, rows // groups, width).astype(
            jnp.bfloat16
        )


def swap(x, axis):
    return lax.all_to_all(x, axis, 0, 0)


def spread(x, axis):
    return swap(jnp.broadcast_to(x[None], (lax.axis_size(axis),) + x.shape), axis)


def per_device(queries, out_grad, branch_kv, trunk_kv, parent, prefix):
    bf16, f32 = jnp.bfloat16, jnp.float32
    width = trunk_kv.shape[1] // 2
    own = queries.shape[1]
    heads = queries.shape[2] // width
    nx, ny = lax.axis_size("x"), lax.axis_size("yh")
    x, yh, core = lax.axis_index("x"), lax.axis_index("yh"), lax.axis_index("c")
    span = trunk_kv.shape[0] * nx
    rows = own * ny
    lanes = rows * heads

    kv = spread(jnp.concatenate([trunk_kv, branch_kv[0]], axis=0), "x")
    qg = spread(jnp.stack([queries[0], out_grad[0]]), "yh")
    q, g = qg[:, 0], qg[:, 1]

    mine = prefix[0].reshape(ny, nx, own)[:, x].reshape(rows)
    lim = jnp.tile(mine - yh * span, heads)[None]
    reach = ancestors_t(parent[0])
    reach = lax.dynamic_slice_in_dim(reach, yh * nx * own, nx * own, 0)
    reach = reach.reshape(nx * own, ny, nx, own)[:, :, x].reshape(nx * own, rows)
    reach = jnp.tile(reach.astype(f32), (1, heads))

    keys = kv.shape[1]
    scratch = [
        pltpu.VMEM((lanes, width), bf16),
        pltpu.VMEM((lanes, width), bf16),
        pltpu.VMEM((keys, lanes), f32),
        pltpu.VMEM((keys, lanes), f32),
    ]
    vmem = pl.BlockSpec(memory_space=pltpu.VMEM)
    stats = pl.pallas_call(
        stats_kernel,
        out_shape=jax.ShapeDtypeStruct((2, lanes), f32),
        in_specs=[vmem] * 5,
        out_specs=vmem,
        scratch_shapes=scratch,
        compiler_params=pltpu.CompilerParams(vmem_limit_bytes=32 << 20),
        name="stats",
    )(lim, reach, q, g, kv)
    stats = spread(stats, "yh")
    pieces = trunk_kv.shape[0] // (2 * own)
    dq, keep, send, tree = pl.pallas_call(
        grads_kernel,
        out_shape=(
            jax.ShapeDtypeStruct((ny, own, heads * width), bf16),
            jax.ShapeDtypeStruct((nx, pieces, own, 2 * width), f32),
            jax.ShapeDtypeStruct((nx, pieces, own, 2 * width), bf16),
            jax.ShapeDtypeStruct((nx, own, 2 * width), f32),
        ),
        in_specs=[pl.BlockSpec(memory_space=pltpu.SMEM)] + [vmem] * 6,
        out_specs=(vmem,) * 4,
        scratch_shapes=scratch
        + [
            pltpu.VMEM((keys, lanes), bf16),
            pltpu.VMEM((keys, lanes), bf16),
            pltpu.VMEM((pieces, 2, own, 2 * width), f32),
            pltpu.VMEM((width, lanes), f32),
        ],
        compiler_params=pltpu.CompilerParams(vmem_limit_bytes=40 << 20),
        name="grads",
    )(core[None], lim, reach, stats, q, g, kv)
    other = lax.ppermute(send, "c", [(0, 1), (1, 0)])
    trunk = (keep + other.astype(f32)).astype(bf16).reshape(nx * pieces, own, 2 * width)
    trunk = jnp.sum(swap(trunk, ("x", "z", "yl")).astype(f32), axis=0)
    query_grad = jnp.sum(swap(dq, "yh").astype(f32), axis=0).astype(bf16)
    branch = jnp.sum(swap(tree, "x"), axis=0)
    return (query_grad[None], branch[None], trunk)


def solution(mesh):
    fine = Mesh(mesh.devices.reshape(4, 4, 8, 2, 2), ("yh", "x") + SET)
    ctx = ("yh", "x")
    return jax.shard_map(
        per_device,
        mesh=fine,
        in_specs=(
            P(SET, ctx, None),
            P(SET, ctx, None),
            P(SET, ctx, None),
            P(ctx, None),
            P(SET, None),
            P(SET, None),
        ),
        out_specs=(P(SET, ctx, None), P(SET, ctx, None), P(ctx + SET, None)),
        check_vma=False,
    )
```

```python
import jax
import jax.numpy as jnp
from jax import lax
from jax.experimental import pallas as pl
from jax.experimental.pallas import tpu as pltpu
from jax.sharding import Mesh, PartitionSpec as P


MASKED = -1e30
TILE = 16
SET = ("z", "yl", "c")


def ancestors_t(parent_row):
    count = parent_row.shape[0]
    labels = jnp.arange(count, dtype=jnp.int32)
    links = (parent_row[None, :] == labels[:, None]) | (labels[:, None] == labels[None, :])
    reach = links.astype(jnp.bfloat16)
    for _ in range(max(count - 1, 1).bit_length()):
        reach = jnp.minimum(jnp.dot(reach, reach, preferred_element_type=jnp.float32), 1.0).astype(
            jnp.bfloat16
        )
    return reach


def dot_nt(left, right):
    return lax.dot_general(
        left, right, (((1,), (1,)), ((), ())), preferred_element_type=jnp.float32
    )


def dot_tn(left, right):
    return lax.dot_general(
        left, right, (((0,), (0,)), ((), ())), preferred_element_type=jnp.float32
    )


def stack_heads(src, which, dst):
    groups, _, own, _ = src.shape
    width = dst.shape[1]
    rows = groups * own
    for h in range(dst.shape[0] // rows):
        for y in range(groups):
            dst[pl.ds(h * rows + y * own, own), :] = src[y, which, :, pl.ds(h * width, width)]


def source(pos_ref, k, blocks):
    return lax.rem(pos_ref[0] + blocks - k, blocks)


def stats_kernel(pos_ref, lim_ref, reach_ref, qg_ref, *refs):
    blocks = 4
    kvs = refs[:blocks]
    out_ref, tops_ref, e_ref, s_ref, qs, gs = refs[blocks:]
    keys, wide = kvs[0].shape
    width = wide // 2
    lanes = qs.shape[0]
    scale = width ** (-0.5)
    trunk = keys - TILE
    stack_heads(qg_ref, 0, qs)
    stack_heads(qg_ref, 1, gs)
    ids = lax.broadcasted_iota(jnp.int32, (TILE, lanes), 0)
    room = jnp.broadcast_to(lim_ref[...], (TILE, lanes)) - ids
    top = jnp.full((1, lanes), MASKED, jnp.float32)
    total = jnp.zeros((1, lanes), jnp.float32)
    slope = jnp.zeros((1, lanes), jnp.float32)
    for k in range(blocks):
        b = source(pos_ref, k, blocks)
        e_ref[k] = dot_nt(kvs[k][:, :width], qs[...])
        s_ref[k] = dot_nt(kvs[k][:, width:], gs[...])

        def mask(t, best):
            at = pl.ds(pl.multiple_of(t * TILE, TILE), TILE)
            s = jnp.where(room > b * trunk + t * TILE, e_ref[k, at, :] * scale, MASKED)
            e_ref[k, at, :] = s
            return jnp.maximum(best, s)

        best = lax.fori_loop(
            0, trunk // TILE, mask, jnp.full((TILE, lanes), MASKED, jnp.float32), unroll=2
        )
        tree = jnp.where(
            reach_ref[pl.ds(pl.multiple_of(b * TILE, TILE), TILE), :] > 0.5,
            e_ref[k, pl.ds(trunk, TILE), :] * scale,
            MASKED,
        )
        e_ref[k, pl.ds(trunk, TILE), :] = tree
        best = jnp.max(jnp.maximum(best, tree), axis=0, keepdims=True)
        now = jnp.maximum(top, best)
        fade = jnp.exp(top - now)
        tops_ref[pl.ds(k, 1), :] = now

        def add(t, sums):
            at = pl.ds(pl.multiple_of(t * TILE, TILE), TILE)
            p = jnp.exp(e_ref[k, at, :] - now)
            e_ref[k, at, :] = p
            return (sums[0] + p, sums[1] + p * s_ref[k, at, :])

        zero = jnp.zeros((TILE, lanes), jnp.float32)
        l, d = lax.fori_loop(0, keys // TILE, add, (zero, zero), unroll=3)
        total = total * fade + jnp.sum(l, axis=0, keepdims=True)
        slope = slope * fade + jnp.sum(d, axis=0, keepdims=True)
        top = now
    out_ref[0:1, :] = top + jnp.log(total)
    out_ref[1:2, :] = slope / total


def grads_kernel(pos_ref, stats_ref, tops_ref, e_ref, s_ref, qs, gs, *refs):
    blocks, keys, lanes = e_ref.shape
    kvs = refs[:blocks]
    qkeep_ref, qsend_ref, keep_ref, send_ref, tkeep_ref, tsend_ref = refs[blocks : blocks + 6]
    d_scr, p_scr, kv_scr, dq_scr, q_scr, tree_scr = refs[blocks + 6 :]
    groups = stats_ref.shape[0]
    own = qkeep_ref.shape[1]
    rows = groups * own
    width = qs.shape[1]
    scale = width ** (-0.5)
    trunk = keys - TILE
    mine = pos_ref[1]
    q_half = lax.div(pos_ref[2], 2)
    tree_half = lax.div(pos_ref[0], 2)
    parts = [stats_ref[i, 0:1, :] for i in range(groups)]
    top = parts[0]
    for part in parts[1:]:
        top = jnp.maximum(top, part)
    total = jnp.zeros_like(top)
    for part in parts:
        total = total + jnp.exp(part - top)
    log_total = top + jnp.log(total)
    delta = jnp.zeros_like(top)
    for i in range(groups):
        delta = delta + jnp.exp(parts[i] - log_total) * stats_ref[i, 1:2, :]
    for k in range(blocks):
        b = source(pos_ref, k, blocks)
        fade = jnp.exp(tops_ref[pl.ds(k, 1), :] - log_total)

        def tile(t, carry):
            at = pl.ds(pl.multiple_of(t * TILE, TILE), TILE)
            p = e_ref[k, at, :] * fade
            d_scr[at, :] = (p * (s_ref[k, at, :] - delta)).astype(jnp.bfloat16)
            p_scr[at, :] = p.astype(jnp.bfloat16)
            return carry

        lax.fori_loop(0, keys // TILE, tile, 0, unroll=3)
        dk = scale * jnp.dot(d_scr[...], qs[...], preferred_element_type=jnp.float32)
        dv = jnp.dot(p_scr[...], gs[...], preferred_element_type=jnp.float32)
        kv_scr[:, :, :, :width] = dk[:trunk].reshape(trunk // (2 * TILE), 2, TILE, width)
        kv_scr[:, :, :, width:] = dv[:trunk].reshape(trunk // (2 * TILE), 2, TILE, width)
        tree_scr[b, :, :width] = dk[trunk:]
        tree_scr[b, :, width:] = dv[trunk:]
        keep_ref[b] = kv_scr[:, mine]
        send_ref[b] = kv_scr[:, 1 - mine].astype(jnp.bfloat16)
        part = dot_tn(kvs[k][:, :width], d_scr[...])
        if k == 0:
            dq_scr[...] = part
        else:
            dq_scr[...] += part
    for h in range(lanes // rows):
        piece = (scale * dq_scr[:, pl.ds(h * rows, rows)]).T
        q_scr[:, :, pl.ds(h * width, width)] = piece.reshape(groups, own, width)
    qkeep_ref[...] = q_scr[pl.ds(2 * q_half, 2)]
    qsend_ref[...] = q_scr[pl.ds(2 - 2 * q_half, 2)].astype(jnp.bfloat16)
    tkeep_ref[...] = tree_scr[pl.ds(2 * tree_half, 2)]
    tsend_ref[...] = tree_scr[pl.ds(2 - 2 * tree_half, 2)]


def swap(x, axis):
    return lax.all_to_all(x, axis, 0, 0)


def spread(x, axis):
    return swap(jnp.broadcast_to(x[None], (lax.axis_size(axis),) + x.shape), axis)


def turn(x, axis, k):
    n = lax.axis_size(axis)
    return lax.ppermute(x, axis, [(i, (i + k) % n) for i in range(n)])


def meet(x, axis, bit):
    return lax.ppermute(x, axis, [(i, i ^ bit) for i in range(lax.axis_size(axis))])


def pick(x, which):
    return lax.dynamic_index_in_dim(x, which, 0, keepdims=False)


def per_device(queries, out_grad, branch_kv, trunk_kv, parent, prefix):
    bf16, f32 = jnp.bfloat16, jnp.float32
    width = trunk_kv.shape[1] // 2
    own = queries.shape[1]
    heads = queries.shape[2] // width
    nx, ny = lax.axis_size("x"), lax.axis_size("yh")
    x, yh, core = lax.axis_index("x"), lax.axis_index("yh"), lax.axis_index("c")
    span = trunk_kv.shape[0] * nx
    rows = own * ny
    lanes = rows * heads
    pos = jnp.stack([x, core, yh])

    qg = spread(jnp.stack([queries[0], out_grad[0]]), "yh")
    kv = jnp.concatenate([trunk_kv, branch_kv[0]], axis=0)
    kvs = [kv] + [turn(kv, "x", k) for k in range(1, nx)]

    mine = prefix[0].reshape(ny, nx, own)[:, x].reshape(rows)
    lim = jnp.tile(mine - yh * span, heads)[None]
    reach = ancestors_t(parent[0])
    reach = lax.dynamic_slice_in_dim(reach, yh * nx * own, nx * own, 0)
    reach = reach.reshape(nx * own, ny, nx, own)[:, :, x].reshape(nx * own, rows)
    reach = jnp.tile(reach.astype(f32), (1, heads))

    keys = kv.shape[0]
    vmem = pl.BlockSpec(memory_space=pltpu.VMEM)
    smem = pl.BlockSpec(memory_space=pltpu.SMEM)
    shape = jax.ShapeDtypeStruct
    stats, tops, e, s, qs, gs = pl.pallas_call(
        stats_kernel,
        out_shape=(
            shape((2, lanes), f32),
            shape((nx, lanes), f32),
            shape((nx, keys, lanes), f32),
            shape((nx, keys, lanes), f32),
            shape((lanes, width), bf16),
            shape((lanes, width), bf16),
        ),
        in_specs=[smem] + [vmem] * (3 + nx),
        out_specs=(vmem,) * 6,
        compiler_params=pltpu.CompilerParams(vmem_limit_bytes=6 << 20),
        name="stats",
    )(pos, lim, reach, qg, *kvs)
    stats = spread(stats, "yh")
    pieces = trunk_kv.shape[0] // (2 * own)
    q_keep, q_send, keep, send, t_keep, t_send = pl.pallas_call(
        grads_kernel,
        out_shape=(
            shape((ny // 2, own, heads * width), f32),
            shape((ny // 2, own, heads * width), bf16),
            shape((nx, pieces, own, 2 * width), f32),
            shape((nx, pieces, own, 2 * width), bf16),
            shape((nx // 2, own, 2 * width), f32),
            shape((nx // 2, own, 2 * width), f32),
        ),
        in_specs=[smem] + [vmem] * (6 + nx),
        out_specs=(vmem,) * 6,
        scratch_shapes=[
            pltpu.VMEM((keys, lanes), bf16),
            pltpu.VMEM((keys, lanes), bf16),
            pltpu.VMEM((pieces, 2, own, 2 * width), f32),
            pltpu.VMEM((width, lanes), f32),
            pltpu.VMEM((ny, own, heads * width), f32),
            pltpu.VMEM((nx, own, 2 * width), f32),
        ],
        compiler_params=pltpu.CompilerParams(vmem_limit_bytes=10 << 20),
        name="grads",
    )(pos, stats, tops, e, s, qs, gs, *kvs)
    other = turn(send, "c", 1)
    trunk = (keep + other.astype(f32)).astype(bf16).reshape(nx * pieces, own, 2 * width)
    trunk = swap(trunk, ("x", "z", "yl"))
    low = lax.rem(yh, 2)
    part = q_keep + meet(q_send, "yh", 2).astype(f32)
    query_grad = pick(part, low) + meet(pick(part, 1 - low).astype(bf16), "yh", 1).astype(f32)
    query_grad = query_grad.astype(bf16)
    low = lax.rem(x, 2)
    part = t_keep + meet(t_send, "x", 2)
    branch = pick(part, low) + meet(pick(part, 1 - low), "x", 1)
    trunk = jnp.sum(trunk.astype(f32), axis=0)
    return (query_grad[None], branch[None], trunk)


def solution(mesh):
    fine = Mesh(mesh.devices.reshape(4, 4, 8, 2, 2), ("yh", "x") + SET)
    ctx = ("yh", "x")
    return jax.shard_map(
        per_device,
        mesh=fine,
        in_specs=(
            P(SET, ctx, None),
            P(SET, ctx, None),
            P(SET, ctx, None),
            P(ctx, None),
            P(SET, None),
            P(SET, None),
        ),
        out_specs=(P(SET, ctx, None), P(SET, ctx, None), P(ctx + SET, None)),
        check_vma=False,
    )
```

```python
import functools

import jax
import jax.numpy as jnp
from jax import lax
from jax.experimental import pallas as pl
from jax.experimental.pallas import tpu as pltpu
from jax.sharding import Mesh, PartitionSpec as P


MASKED = -1e30
TILE = 16
SET = ("z", "yl", "c")


def ancestors_t(parent_row):
    count = parent_row.shape[0]
    labels = jnp.arange(count, dtype=jnp.int32)
    links = (parent_row[None, :] == labels[:, None]) | (labels[:, None] == labels[None, :])
    reach = links.astype(jnp.bfloat16)
    for _ in range(max(count - 1, 1).bit_length()):
        reach = jnp.minimum(jnp.dot(reach, reach, preferred_element_type=jnp.float32), 1.0).astype(
            jnp.bfloat16
        )
    return reach


def dot_nt(left, right):
    return lax.dot_general(
        left, right, (((1,), (1,)), ((), ())), preferred_element_type=jnp.float32
    )


def dot_tn(left, right):
    return lax.dot_general(
        left, right, (((0,), (0,)), ((), ())), preferred_element_type=jnp.float32
    )


def stack_heads(src, which, dst):
    groups, _, own, _ = src.shape
    width = dst.shape[1]
    rows = groups * own
    for h in range(dst.shape[0] // rows):
        for y in range(groups):
            dst[pl.ds(h * rows + y * own, own), :] = src[y, which, :, pl.ds(h * width, width)]


def source(pos_ref, k, blocks):
    return lax.rem(pos_ref[0] + blocks - k, blocks)


def pack_kernel(q_ref, g_ref, trunk_ref, branch_ref, qg_ref, kv_ref, sems):
    copies = [
        pltpu.make_async_copy(part.at[0], qg_ref.at[y, i], sems.at[y, i])
        for y in range(qg_ref.shape[0])
        for i, part in enumerate((q_ref, g_ref))
    ]
    for copy in copies:
        copy.start()
    trunk = trunk_ref.shape[0]
    kv_ref[:trunk, :] = trunk_ref[...]
    kv_ref[trunk:, :] = branch_ref[0]
    for copy in copies:
        copy.wait()


def stats_kernel(shifts, last, pos_ref, lim_ref, reach_ref, *refs):
    count = len(shifts)
    if last:
        qs, gs, before_ref = refs[:3]
        kvs = refs[3 : 3 + count]
        after_ref, tops_ref, e_ref, s_ref = refs[3 + count :]
    else:
        qg_ref = refs[0]
        kvs = refs[1 : 1 + count]
        after_ref, tops_ref, e_ref, s_ref, qs, gs = refs[1 + count :]
        stack_heads(qg_ref, 0, qs)
        stack_heads(qg_ref, 1, gs)
    keys, wide = kvs[0].shape
    width = wide // 2
    lanes = qs.shape[0]
    scale = width ** (-0.5)
    trunk = keys - TILE
    ids = lax.broadcasted_iota(jnp.int32, (TILE, lanes), 0)
    room = jnp.broadcast_to(lim_ref[...], (TILE, lanes)) - ids
    if last:
        top, total, slope = (before_ref[i : i + 1, :] for i in range(3))
    else:
        top = jnp.full((1, lanes), MASKED, jnp.float32)
        total = jnp.zeros((1, lanes), jnp.float32)
        slope = jnp.zeros((1, lanes), jnp.float32)
    for i in range(count):
        b = source(pos_ref, shifts[i], 4)
        e_ref[i] = dot_nt(kvs[i][:, :width], qs[...])
        s_ref[i] = dot_nt(kvs[i][:, width:], gs[...])

        def mask(t, best):
            at = pl.ds(pl.multiple_of(t * TILE, TILE), TILE)
            s = jnp.where(room > b * trunk + t * TILE, e_ref[i, at, :] * scale, MASKED)
            e_ref[i, at, :] = s
            return jnp.maximum(best, s)

        best = lax.fori_loop(
            0, trunk // TILE, mask, jnp.full((TILE, lanes), MASKED, jnp.float32), unroll=2
        )
        tree = jnp.where(
            reach_ref[pl.ds(pl.multiple_of(b * TILE, TILE), TILE), :] > 0.5,
            e_ref[i, pl.ds(trunk, TILE), :] * scale,
            MASKED,
        )
        e_ref[i, pl.ds(trunk, TILE), :] = tree
        best = jnp.max(jnp.maximum(best, tree), axis=0, keepdims=True)
        now = jnp.maximum(top, best)
        fade = jnp.exp(top - now)
        tops_ref[pl.ds(i, 1), :] = now

        def add(t, sums):
            at = pl.ds(pl.multiple_of(t * TILE, TILE), TILE)
            p = jnp.exp(e_ref[i, at, :] - now)
            e_ref[i, at, :] = p
            return (sums[0] + p, sums[1] + p * s_ref[i, at, :])

        zero = jnp.zeros((TILE, lanes), jnp.float32)
        l, d = lax.fori_loop(0, keys // TILE, add, (zero, zero), unroll=3)
        total = total * fade + jnp.sum(l, axis=0, keepdims=True)
        slope = slope * fade + jnp.sum(d, axis=0, keepdims=True)
        top = now
    if last:
        after_ref[0:1, :] = top + jnp.log(total)
        after_ref[1:2, :] = slope / total
    else:
        after_ref[0:1, :] = top
        after_ref[1:2, :] = total
        after_ref[2:3, :] = slope


def grads_kernel(shifts, pos_ref, stats_ref, qs, gs, *refs):
    blocks = len(shifts[0]) + len(shifts[1])
    kvs = refs[6 : 6 + blocks]
    held = [
        (k, kvs[k], refs[3 * half].at[pl.ds(i, 1)], refs[3 * half + 1].at[i], refs[3 * half + 2].at[i])
        for half in range(2)
        for i, k in enumerate(shifts[half])
    ]
    qkeep_ref, qsend_ref, keep_ref, send_ref, tkeep_ref, tsend_ref = refs[6 + blocks : 12 + blocks]
    d_scr, p_scr, kv_scr, dq_scr, q_scr, tree_scr = refs[12 + blocks :]
    keys, lanes = d_scr.shape
    groups = stats_ref.shape[0]
    own = qkeep_ref.shape[1]
    rows = groups * own
    width = qs.shape[1]
    scale = width ** (-0.5)
    trunk = keys - TILE
    mine = pos_ref[1]
    q_half = lax.div(pos_ref[2], 2)
    tree_half = lax.div(pos_ref[0], 2)
    parts = [stats_ref[i, 0:1, :] for i in range(groups)]
    top = parts[0]
    for part in parts[1:]:
        top = jnp.maximum(top, part)
    total = jnp.zeros_like(top)
    for part in parts:
        total = total + jnp.exp(part - top)
    log_total = top + jnp.log(total)
    delta = jnp.zeros_like(top)
    for i in range(groups):
        delta = delta + jnp.exp(parts[i] - log_total) * stats_ref[i, 1:2, :]
    for step, (k, kv_ref, top_ref, e_ref, s_ref) in enumerate(held):
        b = source(pos_ref, k, blocks)
        fade = jnp.exp(top_ref[...] - log_total)

        def tile(t, carry):
            at = pl.ds(pl.multiple_of(t * TILE, TILE), TILE)
            p = e_ref[at, :] * fade
            d_scr[at, :] = (p * (s_ref[at, :] - delta)).astype(jnp.bfloat16)
            p_scr[at, :] = p.astype(jnp.bfloat16)
            return carry

        lax.fori_loop(0, keys // TILE, tile, 0, unroll=3)
        dk = scale * jnp.dot(d_scr[...], qs[...], preferred_element_type=jnp.float32)
        dv = jnp.dot(p_scr[...], gs[...], preferred_element_type=jnp.float32)
        kv_scr[:, :, :, :width] = dk[:trunk].reshape(trunk // (2 * TILE), 2, TILE, width)
        kv_scr[:, :, :, width:] = dv[:trunk].reshape(trunk // (2 * TILE), 2, TILE, width)
        tree_scr[b, :, :width] = dk[trunk:]
        tree_scr[b, :, width:] = dv[trunk:]
        keep_ref[b] = kv_scr[:, mine]
        send_ref[b] = kv_scr[:, 1 - mine].astype(jnp.bfloat16)
        part = dot_tn(kv_ref[:, :width], d_scr[...])
        if step == 0:
            dq_scr[...] = part
        else:
            dq_scr[...] += part
    for h in range(lanes // rows):
        piece = (scale * dq_scr[:, pl.ds(h * rows, rows)]).T
        q_scr[:, :, pl.ds(h * width, width)] = piece.reshape(groups, own, width)
    qkeep_ref[...] = q_scr[pl.ds(2 * q_half, 2)]
    qsend_ref[...] = q_scr[pl.ds(2 - 2 * q_half, 2)].astype(jnp.bfloat16)
    tkeep_ref[...] = tree_scr[pl.ds(2 * tree_half, 2)]
    tsend_ref[...] = tree_scr[pl.ds(2 - 2 * tree_half, 2)]


def swap(x, axis):
    return lax.all_to_all(x, axis, 0, 0)


def spread(x, axis):
    return swap(jnp.broadcast_to(x[None], (lax.axis_size(axis),) + x.shape), axis)


def turn(x, axis, k):
    n = lax.axis_size(axis)
    return lax.ppermute(x, axis, [(i, (i + k) % n) for i in range(n)])


def meet(x, axis, bit):
    return lax.ppermute(x, axis, [(i, i ^ bit) for i in range(lax.axis_size(axis))])


def pick(x, which):
    return lax.dynamic_index_in_dim(x, which, 0, keepdims=False)


def per_device(queries, out_grad, branch_kv, trunk_kv, parent, prefix):
    bf16, f32 = jnp.bfloat16, jnp.float32
    width = trunk_kv.shape[1] // 2
    own = queries.shape[1]
    heads = queries.shape[2] // width
    nx, ny = lax.axis_size("x"), lax.axis_size("yh")
    x, yh, core = lax.axis_index("x"), lax.axis_index("yh"), lax.axis_index("c")
    span = trunk_kv.shape[0] * nx
    rows = own * ny
    lanes = rows * heads
    pos = jnp.stack([x, core, yh])

    shape = jax.ShapeDtypeStruct
    vmem = pl.BlockSpec(memory_space=pltpu.VMEM)
    smem = pl.BlockSpec(memory_space=pltpu.SMEM)
    qg, kv = pl.pallas_call(
        pack_kernel,
        out_shape=(
            shape((ny, 2) + queries.shape[1:], bf16),
            shape((trunk_kv.shape[0] + own, 2 * width), bf16),
        ),
        in_specs=[vmem] * 4,
        out_specs=(pl.BlockSpec(memory_space=pl.ANY), vmem),
        scratch_shapes=[pltpu.SemaphoreType.DMA((ny, 2))],
        compiler_params=pltpu.CompilerParams(vmem_limit_bytes=4 << 20),
        name="pack",
    )(queries, out_grad, trunk_kv, branch_kv)
    qg = swap(qg, "yh")
    kvs = [kv] + [turn(kv, "x", k) for k in range(1, nx)]
    shifts = ((0, 1), (2, 3))

    mine = prefix[0].reshape(ny, nx, own)[:, x].reshape(rows)
    lim = jnp.tile(mine - yh * span, heads)[None]
    reach = ancestors_t(parent[0])
    reach = lax.dynamic_slice_in_dim(reach, yh * nx * own, nx * own, 0)
    reach = reach.reshape(nx * own, ny, nx, own)[:, :, x].reshape(nx * own, rows)
    reach = jnp.tile(reach.astype(f32), (1, heads))

    keys = kv.shape[0]
    head = (pos, lim, reach)
    rest = [qg]
    held = []
    for half in range(2):
        count = len(shifts[half])
        outs = [
            shape((3 - half, lanes), f32),
            shape((count, lanes), f32),
            shape((count, keys, lanes), f32),
            shape((count, keys, lanes), f32),
        ]
        if half == 0:
            outs += [shape((lanes, width), bf16)] * 2
        stats, tops, e, s, *stacked = pl.pallas_call(
            functools.partial(stats_kernel, shifts[half], half == 1),
            out_shape=tuple(outs),
            in_specs=[smem] + [vmem] * (2 + len(rest) + count),
            out_specs=(vmem,) * len(outs),
            compiler_params=pltpu.CompilerParams(vmem_limit_bytes=6 << 20),
            name="stats",
        )(*head, *rest, *[kvs[k] for k in shifts[half]])
        held += [tops, e, s]
        if half == 0:
            qs, gs = stacked
            rest = [qs, gs, stats]
    stats = spread(stats, "yh")
    pieces = trunk_kv.shape[0] // (2 * own)
    q_keep, q_send, keep, send, t_keep, t_send = pl.pallas_call(
        functools.partial(grads_kernel, shifts),
        out_shape=(
            shape((ny // 2, own, heads * width), f32),
            shape((ny // 2, own, heads * width), bf16),
            shape((nx, pieces, own, 2 * width), f32),
            shape((nx, pieces, own, 2 * width), bf16),
            shape((nx // 2, own, 2 * width), f32),
            shape((nx // 2, own, 2 * width), f32),
        ),
        in_specs=[smem] + [vmem] * (9 + nx),
        out_specs=(vmem,) * 6,
        scratch_shapes=[
            pltpu.VMEM((keys, lanes), bf16),
            pltpu.VMEM((keys, lanes), bf16),
            pltpu.VMEM((pieces, 2, own, 2 * width), f32),
            pltpu.VMEM((width, lanes), f32),
            pltpu.VMEM((ny, own, heads * width), f32),
            pltpu.VMEM((nx, own, 2 * width), f32),
        ],
        compiler_params=pltpu.CompilerParams(vmem_limit_bytes=10 << 20),
        name="grads",
    )(pos, stats, qs, gs, *held, *kvs)
    other = turn(send, "c", 1)
    trunk = (keep + other.astype(f32)).astype(bf16).reshape(nx * pieces, own, 2 * width)
    trunk = swap(trunk, ("x", "z", "yl"))
    low = lax.rem(yh, 2)
    part = q_keep + meet(q_send, "yh", 2).astype(f32)
    query_grad = pick(part, low) + meet(pick(part, 1 - low).astype(bf16), "yh", 1).astype(f32)
    query_grad = query_grad.astype(bf16)
    low = lax.rem(x, 2)
    part = t_keep + meet(t_send, "x", 2)
    branch = pick(part, low) + meet(pick(part, 1 - low), "x", 1)
    trunk = jnp.sum(trunk.astype(f32), axis=0)
    return (query_grad[None], branch[None], trunk)


def solution(mesh):
    fine = Mesh(mesh.devices.reshape(4, 4, 8, 2, 2), ("yh", "x") + SET)
    ctx = ("yh", "x")
    return jax.shard_map(
        per_device,
        mesh=fine,
        in_specs=(
            P(SET, ctx, None),
            P(SET, ctx, None),
            P(SET, ctx, None),
            P(ctx, None),
            P(SET, None),
            P(SET, None),
        ),
        out_specs=(P(SET, ctx, None), P(SET, ctx, None), P(ctx + SET, None)),
        check_vma=False,
    )
```

```python
import functools

import jax
import jax.numpy as jnp
from jax import lax
from jax.experimental import pallas as pl
from jax.experimental.pallas import tpu as pltpu
from jax.sharding import Mesh, PartitionSpec as P


MASKED = -1e30
TILE = 16
SET = ("z", "yl", "c")


def ancestors_t(parent_row):
    count = parent_row.shape[0]
    labels = jnp.arange(count, dtype=jnp.int32)
    links = (parent_row[None, :] == labels[:, None]) | (labels[:, None] == labels[None, :])
    reach = links.astype(jnp.bfloat16)
    for _ in range(max(count - 1, 1).bit_length()):
        reach = jnp.minimum(jnp.dot(reach, reach, preferred_element_type=jnp.float32), 1.0).astype(
            jnp.bfloat16
        )
    return reach


def dot_nt(left, right):
    return lax.dot_general(
        left, right, (((1,), (1,)), ((), ())), preferred_element_type=jnp.float32
    )


def dot_tn(left, right):
    return lax.dot_general(
        left, right, (((0,), (0,)), ((), ())), preferred_element_type=jnp.float32
    )


def stack_heads(src, which, dst):
    groups, _, own, _ = src.shape
    width = dst.shape[1]
    rows = groups * own
    for h in range(dst.shape[0] // rows):
        for y in range(groups):
            dst[pl.ds(h * rows + y * own, own), :] = src[y, which, :, pl.ds(h * width, width)]


def source(pos_ref, k, blocks):
    return lax.rem(pos_ref[0] + blocks - k, blocks)


def pack_kernel(q_ref, g_ref, trunk_ref, branch_ref, qg_ref, kv_ref, held, load_sems, sems):
    trunk = trunk_ref.shape[0]
    loads = [
        pltpu.make_async_copy(q_ref.at[0], held.at[0], load_sems.at[0]),
        pltpu.make_async_copy(g_ref.at[0], held.at[1], load_sems.at[1]),
        pltpu.make_async_copy(trunk_ref, kv_ref.at[pl.ds(0, trunk)], load_sems.at[2]),
        pltpu.make_async_copy(
            branch_ref.at[0], kv_ref.at[pl.ds(trunk, branch_ref.shape[1])], load_sems.at[3]
        ),
    ]
    for load in loads:
        load.start()
    stores = []
    for i in range(2):
        loads[i].wait()
        for y in range(qg_ref.shape[0]):
            stores.append(pltpu.make_async_copy(held.at[i], qg_ref.at[y, i], sems.at[y, i]))
            stores[-1].start()
    for load in loads[2:]:
        load.wait()
    for store in stores:
        store.wait()


def stats_kernel(shifts, last, pos_ref, lim_ref, reach_ref, *refs):
    count = len(shifts)
    if last:
        qs, gs, before_ref = refs[:3]
        kvs = refs[3 : 3 + count]
        after_ref, tops_ref, e_ref, s_ref = refs[3 + count :]
    else:
        qg_ref = refs[0]
        kvs = refs[1 : 1 + count]
        after_ref, tops_ref, e_ref, s_ref, qs, gs = refs[1 + count :]
        stack_heads(qg_ref, 0, qs)
        stack_heads(qg_ref, 1, gs)
    keys, wide = kvs[0].shape
    width = wide // 2
    lanes = qs.shape[0]
    scale = width ** (-0.5)
    trunk = keys - TILE
    ids = lax.broadcasted_iota(jnp.int32, (TILE, lanes), 0)
    room = jnp.broadcast_to(lim_ref[...], (TILE, lanes)) - ids
    if last:
        top, total, slope = (before_ref[i : i + 1, :] for i in range(3))
    else:
        top = jnp.full((1, lanes), MASKED, jnp.float32)
        total = jnp.zeros((1, lanes), jnp.float32)
        slope = jnp.zeros((1, lanes), jnp.float32)
    for i in range(count):
        b = source(pos_ref, shifts[i], 4)
        e_ref[i] = dot_nt(kvs[i][:, :width], qs[...])
        s_ref[i] = dot_nt(kvs[i][:, width:], gs[...])

        def mask(t, best):
            at = pl.ds(pl.multiple_of(t * TILE, TILE), TILE)
            s = jnp.where(room > b * trunk + t * TILE, e_ref[i, at, :] * scale, MASKED)
            e_ref[i, at, :] = s
            return jnp.maximum(best, s)

        best = lax.fori_loop(
            0, trunk // TILE, mask, jnp.full((TILE, lanes), MASKED, jnp.float32), unroll=2
        )
        tree = jnp.where(
            reach_ref[pl.ds(pl.multiple_of(b * TILE, TILE), TILE), :] > 0.5,
            e_ref[i, pl.ds(trunk, TILE), :] * scale,
            MASKED,
        )
        e_ref[i, pl.ds(trunk, TILE), :] = tree
        best = jnp.max(jnp.maximum(best, tree), axis=0, keepdims=True)
        now = jnp.maximum(top, best)
        fade = jnp.exp(top - now)
        tops_ref[pl.ds(i, 1), :] = now

        def add(t, sums):
            at = pl.ds(pl.multiple_of(t * TILE, TILE), TILE)
            p = jnp.exp(e_ref[i, at, :] - now)
            e_ref[i, at, :] = p
            return (sums[0] + p, sums[1] + p * s_ref[i, at, :])

        zero = jnp.zeros((TILE, lanes), jnp.float32)
        l, d = lax.fori_loop(0, keys // TILE, add, (zero, zero), unroll=3)
        total = total * fade + jnp.sum(l, axis=0, keepdims=True)
        slope = slope * fade + jnp.sum(d, axis=0, keepdims=True)
        top = now
    if last:
        after_ref[0:1, :] = top + jnp.log(total)
        after_ref[1:2, :] = slope / total
    else:
        after_ref[0:1, :] = top
        after_ref[1:2, :] = total
        after_ref[2:3, :] = slope


def grads_kernel(shifts, pos_ref, stats_ref, qs, gs, *refs):
    blocks = len(shifts[0]) + len(shifts[1])
    kvs = refs[6 : 6 + blocks]
    held = [
        (k, kvs[k], refs[3 * half].at[pl.ds(i, 1)], refs[3 * half + 1].at[i], refs[3 * half + 2].at[i])
        for half in range(2)
        for i, k in enumerate(shifts[half])
    ]
    qkeep_ref, qsend_ref, part_ref = refs[6 + blocks : 9 + blocks]
    d_scr, p_scr, part_scr, dq_scr, q_scr, sems = refs[9 + blocks :]
    keys, lanes = d_scr.shape
    groups = stats_ref.shape[0]
    own = qkeep_ref.shape[1]
    rows = groups * own
    width = qs.shape[1]
    scale = width ** (-0.5)
    trunk = keys - TILE
    mine = pos_ref[1]
    q_half = lax.div(pos_ref[2], 2)
    parts = [stats_ref[i, 0:1, :] for i in range(groups)]
    top = parts[0]
    for part in parts[1:]:
        top = jnp.maximum(top, part)
    total = jnp.zeros_like(top)
    for part in parts:
        total = total + jnp.exp(part - top)
    log_total = top + jnp.log(total)
    delta = jnp.zeros_like(top)
    for i in range(groups):
        delta = delta + jnp.exp(parts[i] - log_total) * stats_ref[i, 1:2, :]
    copies = []
    for step, (k, kv_ref, top_ref, e_ref, s_ref) in enumerate(held):
        b = source(pos_ref, k, blocks)
        fade = jnp.exp(top_ref[...] - log_total)

        def tile(t, carry):
            at = pl.ds(pl.multiple_of(t * TILE, TILE), TILE)
            p = e_ref[at, :] * fade
            d_scr[at, :] = (p * (s_ref[at, :] - delta)).astype(jnp.bfloat16)
            p_scr[at, :] = p.astype(jnp.bfloat16)
            return carry

        lax.fori_loop(0, keys // TILE, tile, 0, unroll=3)
        dk = scale * jnp.dot(d_scr[...], qs[...], preferred_element_type=jnp.float32)
        dv = jnp.dot(p_scr[...], gs[...], preferred_element_type=jnp.float32)
        for half, grad in enumerate((dk, dv)):
            at = pl.ds(half * width, width)
            grad = grad.astype(jnp.bfloat16)
            for piece in range(trunk // TILE):
                part_scr[step, piece % 2, pl.ds(piece // 2 * TILE, TILE), at] = grad[
                    piece * TILE : (piece + 1) * TILE
                ]
            for core in range(2):
                part_scr[step, core, pl.ds(trunk // 2, TILE), at] = jnp.where(
                    core == mine, grad[trunk:], jnp.zeros_like(grad[trunk:])
                )
        copies.append(pltpu.make_async_copy(part_scr.at[step], part_ref.at[b], sems.at[step]))
        copies[-1].start()
        part = dot_tn(kv_ref[:, :width], d_scr[...])
        if step == 0:
            dq_scr[...] = part
        else:
            dq_scr[...] += part
    for h in range(lanes // rows):
        piece = (scale * dq_scr[:, pl.ds(h * rows, rows)]).T
        q_scr[:, :, pl.ds(h * width, width)] = piece.reshape(groups, own, width)
    qkeep_ref[...] = q_scr[pl.ds(2 * q_half, 2)]
    qsend_ref[...] = q_scr[pl.ds(2 - 2 * q_half, 2)].astype(jnp.bfloat16)
    for copy in copies:
        copy.wait()


def swap(x, axis):
    return lax.all_to_all(x, axis, 0, 0)


def spread(x, axis):
    return swap(jnp.broadcast_to(x[None], (lax.axis_size(axis),) + x.shape), axis)


def turn(x, axis, k):
    n = lax.axis_size(axis)
    return lax.ppermute(x, axis, [(i, (i + k) % n) for i in range(n)])


def meet(x, axis, bit):
    return lax.ppermute(x, axis, [(i, i ^ bit) for i in range(lax.axis_size(axis))])


def pick(x, which):
    return lax.dynamic_index_in_dim(x, which, 0, keepdims=False)


def per_device(queries, out_grad, branch_kv, trunk_kv, parent, prefix):
    bf16, f32 = jnp.bfloat16, jnp.float32
    width = trunk_kv.shape[1] // 2
    own = queries.shape[1]
    heads = queries.shape[2] // width
    nx, ny = lax.axis_size("x"), lax.axis_size("yh")
    x, yh, core = lax.axis_index("x"), lax.axis_index("yh"), lax.axis_index("c")
    span = trunk_kv.shape[0] * nx
    rows = own * ny
    lanes = rows * heads
    pos = jnp.stack([x, core, yh])

    shape = jax.ShapeDtypeStruct
    vmem = pl.BlockSpec(memory_space=pltpu.VMEM)
    smem = pl.BlockSpec(memory_space=pltpu.SMEM)
    anywhere = pl.BlockSpec(memory_space=pl.ANY)
    qg, kv = pl.pallas_call(
        pack_kernel,
        out_shape=(
            shape((ny, 2) + queries.shape[1:], bf16),
            shape((trunk_kv.shape[0] + own, 2 * width), bf16),
        ),
        in_specs=[anywhere] * 4,
        out_specs=(anywhere, vmem),
        scratch_shapes=[
            pltpu.VMEM((2,) + queries.shape[1:], bf16),
            pltpu.SemaphoreType.DMA((4,)),
            pltpu.SemaphoreType.DMA((ny, 2)),
        ],
        name="pack",
    )(queries, out_grad, trunk_kv, branch_kv)
    qg = swap(qg, "yh")
    kvs = [kv] + [turn(kv, "x", k) for k in range(1, nx)]
    shifts = ((0, 1), (2, 3))

    mine = prefix[0].reshape(ny, nx, own)[:, x].reshape(rows)
    lim = jnp.tile(mine - yh * span, heads)[None]
    reach = ancestors_t(parent[0])
    reach = lax.dynamic_slice_in_dim(reach, yh * nx * own, nx * own, 0)
    reach = reach.reshape(nx * own, ny, nx, own)[:, :, x].reshape(nx * own, rows)
    reach = jnp.tile(reach.astype(f32), (1, heads))

    keys = kv.shape[0]
    head = (pos, lim, reach)
    rest = [qg]
    held = []
    for half in range(2):
        count = len(shifts[half])
        outs = [
            shape((3 - half, lanes), f32),
            shape((count, lanes), f32),
            shape((count, keys, lanes), f32),
            shape((count, keys, lanes), f32),
        ]
        if half == 0:
            outs += [shape((lanes, width), bf16)] * 2
        stats, tops, e, s, *stacked = pl.pallas_call(
            functools.partial(stats_kernel, shifts[half], half == 1),
            out_shape=tuple(outs),
            in_specs=[smem] + [vmem] * (2 + len(rest) + count),
            out_specs=(vmem,) * len(outs),
            compiler_params=pltpu.CompilerParams(vmem_limit_bytes=6 << 20),
            name="stats",
        )(*head, *rest, *[kvs[k] for k in shifts[half]])
        held += [tops, e, s]
        if half == 0:
            qs, gs = stacked
            rest = [qs, gs, stats]
    stats = spread(stats, "yh")
    half_keys = trunk_kv.shape[0] // 2
    q_keep, q_send, part = pl.pallas_call(
        functools.partial(grads_kernel, shifts),
        out_shape=(
            shape((ny // 2, own, heads * width), f32),
            shape((ny // 2, own, heads * width), bf16),
            shape((nx, 2, half_keys + own, 2 * width), bf16),
        ),
        in_specs=[smem] + [vmem] * (9 + nx),
        out_specs=(vmem, vmem, anywhere),
        scratch_shapes=[
            pltpu.VMEM((keys, lanes), bf16),
            pltpu.VMEM((keys, lanes), bf16),
            pltpu.VMEM((nx, 2, half_keys + own, 2 * width), bf16),
            pltpu.VMEM((width, lanes), f32),
            pltpu.VMEM((ny, own, heads * width), f32),
            pltpu.SemaphoreType.DMA((nx,)),
        ],
        compiler_params=pltpu.CompilerParams(vmem_limit_bytes=10 << 20),
        name="grads",
    )(pos, stats, qs, gs, *held, *kvs)
    part = swap(part.reshape(nx * 2, half_keys + own, 2 * width), ("x", "c"))
    part = jnp.sum(part.astype(f32), axis=0)
    branch = part[half_keys:]
    trunk = part[:half_keys].astype(bf16).reshape(half_keys // own, own, 2 * width)
    trunk = swap(trunk, ("z", "yl"))
    low = lax.rem(yh, 2)
    part = q_keep + meet(q_send, "yh", 2).astype(f32)
    query_grad = pick(part, low) + meet(pick(part, 1 - low).astype(bf16), "yh", 1).astype(f32)
    query_grad = query_grad.astype(bf16)
    trunk = jnp.sum(trunk.astype(f32), axis=0)
    return (query_grad[None], branch[None], trunk)


def solution(mesh):
    fine = Mesh(mesh.devices.reshape(4, 4, 8, 2, 2), ("yh", "x") + SET)
    ctx = ("yh", "x")
    return jax.shard_map(
        per_device,
        mesh=fine,
        in_specs=(
            P(SET, ctx, None),
            P(SET, ctx, None),
            P(SET, ctx, None),
            P(ctx, None),
            P(SET, None),
            P(SET, None),
        ),
        out_specs=(P(SET, ctx, None), P(SET, ctx, None), P(ctx + SET, None)),
        check_vma=False,
    )
```

```python
import functools
import math

import jax
import jax.numpy as jnp
from jax import lax
from jax.experimental import pallas as pl
from jax.experimental.pallas import tpu as pltpu
from jax.sharding import Mesh, PartitionSpec as P


MASKED = -1e30
TILE = 16
STRIP = 8
SET = ("z", "yl", "c")


def dot_nt(left, right):
    return lax.dot_general(
        left, right, (((1,), (1,)), ((), ())), preferred_element_type=jnp.float32
    )


def dot_tn(left, right):
    return lax.dot_general(
        left, right, (((0,), (0,)), ((), ())), preferred_element_type=jnp.float32
    )


def stack_heads(src, which, dst):
    groups, _, own, _ = src.shape
    width = dst.shape[1]
    rows = groups * own
    for h in range(dst.shape[0] // rows):
        for y in range(groups):
            dst[pl.ds(h * rows + y * own, own), :] = src[y, which, :, pl.ds(h * width, width)]


def source(pos_ref, k, blocks):
    return lax.rem(pos_ref[0] + blocks - k, blocks)


def pack_kernel(q_ref, g_ref, trunk_ref, branch_ref, qg_ref, kv_ref, held, load_sems, sems):
    trunk = trunk_ref.shape[0]
    loads = [
        pltpu.make_async_copy(q_ref.at[0], held.at[0], load_sems.at[0]),
        pltpu.make_async_copy(g_ref.at[0], held.at[1], load_sems.at[1]),
        pltpu.make_async_copy(trunk_ref, kv_ref.at[pl.ds(0, trunk)], load_sems.at[2]),
        pltpu.make_async_copy(
            branch_ref.at[0], kv_ref.at[pl.ds(trunk, branch_ref.shape[1])], load_sems.at[3]
        ),
    ]
    for load in loads:
        load.start()
    stores = []
    for i in range(2):
        loads[i].wait()
        for y in range(qg_ref.shape[0]):
            stores.append(pltpu.make_async_copy(held.at[i], qg_ref.at[y, i], sems.at[y, i]))
            stores[-1].start()
    for load in loads[2:]:
        load.wait()
    for store in stores:
        store.wait()


def masks_kernel(nx, own, span, pos_ref, parent_ref, prefix_ref, lim_ref, reach_ref, closed):
    count = parent_ref.shape[1]
    lanes = lim_ref.shape[1]
    x, yh = pos_ref[0], pos_ref[2]
    above = lax.broadcasted_iota(jnp.int32, (count, count), 0)
    below = lax.broadcasted_iota(jnp.int32, (count, count), 1)
    reach = jnp.where((parent_ref[...] == above) | (above == below), 1.0, 0.0).astype(jnp.bfloat16)
    for _ in range(max(count - 1, 1).bit_length()):
        pairs = jnp.dot(reach, reach, preferred_element_type=jnp.float32)
        reach = jnp.minimum(pairs, 1.0).astype(jnp.bfloat16)
    closed[...] = reach.astype(jnp.float32)
    rows = count // nx
    lane = lax.broadcasted_iota(jnp.int32, (count, lanes), 1)
    row = lax.rem(lax.div(lane, own), rows // own) * (nx * own) + x * own + lax.rem(lane, own)
    chosen = jnp.where(lax.broadcasted_iota(jnp.int32, (count, lanes), 0) == row, 1.0, 0.0)
    chosen = chosen.astype(jnp.bfloat16)
    mine = closed[pl.ds(pl.multiple_of(yh * nx * own, nx * own), nx * own), :]
    reach_ref[...] = jnp.dot(mine.astype(jnp.bfloat16), chosen, preferred_element_type=jnp.float32)
    prefix = prefix_ref[...]
    part = lax.broadcasted_iota(jnp.int32, (TILE, count), 0)
    digits = jnp.where(part == 0, lax.div(prefix, 128), lax.rem(prefix, 128))
    digits = jnp.dot(
        digits.astype(jnp.float32).astype(jnp.bfloat16), chosen, preferred_element_type=jnp.float32
    )
    lim = (digits[0:1] * 128.0 + digits[1:2]).astype(jnp.int32)
    lim_ref[...] = lim - yh * span


def stats_kernel(shifts, last, pos_ref, lim_ref, reach_ref, *refs):
    count = len(shifts)
    if last:
        qs, gs, before_ref = refs[:3]
        kvs = refs[3 : 3 + count]
        after_ref, tops_ref, e_ref, s_ref = refs[3 + count :]
    else:
        qg_ref = refs[0]
        kvs = refs[1 : 1 + count]
        after_ref, tops_ref, e_ref, s_ref, qs, gs = refs[1 + count :]
        stack_heads(qg_ref, 0, qs)
        stack_heads(qg_ref, 1, gs)
    keys, wide = kvs[0].shape
    width = wide // 2
    lanes = qs.shape[0]
    scale = width ** (-0.5)
    trunk = keys - TILE
    power = scale * math.log2(math.e)
    ids = lax.broadcasted_iota(jnp.int32, (trunk, lanes), 0)
    if last:
        top, total, slope = (before_ref[i : i + 1, :] for i in range(3))
    else:
        top = jnp.full((1, lanes), MASKED, jnp.float32)
        total = jnp.zeros((1, lanes), jnp.float32)
        slope = jnp.zeros((1, lanes), jnp.float32)
    nows = []

    def score(i):
        b = source(pos_ref, shifts[i], 4)
        raw = dot_nt(kvs[i][:, :width], qs[...])
        near = jnp.where(ids < lim_ref[...] - b * trunk, raw[:trunk], MASKED)
        tree = jnp.where(
            reach_ref[pl.ds(pl.multiple_of(b * TILE, TILE), TILE), :] > 0.5, raw[trunk:], MASKED
        )
        e_ref[i, :trunk, :] = near
        e_ref[i, trunk:, :] = tree
        best = jnp.maximum(
            jnp.max(near, axis=0, keepdims=True), jnp.max(tree, axis=0, keepdims=True)
        )
        s_ref[i] = dot_nt(kvs[i][:, width:], gs[...])
        nows.append(jnp.maximum(nows[-1] if nows else top, best))
        tops_ref[pl.ds(i, 1), :] = nows[-1] * scale

    def weigh(i, total, slope):
        now = nows[i]
        fade = jnp.exp2(((nows[i - 1] if i else top) - now) * power)
        l = jnp.zeros((STRIP, lanes), jnp.float32)
        d = jnp.zeros((STRIP, lanes), jnp.float32)
        for t in range(keys // STRIP):
            at = pl.ds(t * STRIP, STRIP)
            p = jnp.exp2((e_ref[i, at, :] - now) * power)
            l = l + p
            d = d + p * s_ref[i, at, :]
            e_ref[i, at, :] = p
        return (
            total * fade + jnp.sum(l, axis=0, keepdims=True),
            slope * fade + jnp.sum(d, axis=0, keepdims=True),
        )

    for i in range(count):
        score(i)
    for i in range(count):
        total, slope = weigh(i, total, slope)
    top = nows[-1]
    if last:
        after_ref[0:1, :] = top * scale + jnp.log(total)
        after_ref[1:2, :] = slope / total
    else:
        after_ref[0:1, :] = top
        after_ref[1:2, :] = total
        after_ref[2:3, :] = slope


def grads_kernel(shifts, pos_ref, stats_ref, qs, gs, *refs):
    blocks = len(shifts[0]) + len(shifts[1])
    kvs = refs[6 : 6 + blocks]
    held = [
        (k, kvs[k], refs[3 * half].at[pl.ds(i, 1)], refs[3 * half + 1].at[i], refs[3 * half + 2].at[i])
        for half in range(2)
        for i, k in enumerate(shifts[half])
    ]
    qkeep_ref, qsend_ref, keep_ref, send_ref, tkeep_ref, tsend_ref = refs[6 + blocks : 12 + blocks]
    d_scr, p_scr, tree_d, tree_k, kv_scr, tree_scr, dq_scr, q_scr = refs[12 + blocks :]
    _, keys, lanes = d_scr.shape
    groups = stats_ref.shape[0]
    own = qkeep_ref.shape[1]
    rows = groups * own
    width = qs.shape[1]
    scale = width ** (-0.5)
    trunk = keys - TILE
    mine = pos_ref[1]
    q_low = lax.rem(pos_ref[2], 2)
    tree_low = lax.rem(pos_ref[0], 2)
    parts = [stats_ref[i, 0:1, :] for i in range(groups)]
    top = parts[0]
    for part in parts[1:]:
        top = jnp.maximum(top, part)
    total = jnp.zeros_like(top)
    for part in parts:
        total = total + jnp.exp(part - top)
    log_total = top + jnp.log(total)
    delta = jnp.zeros_like(top)
    for i in range(groups):
        delta = delta + jnp.exp(parts[i] - log_total) * stats_ref[i, 1:2, :]

    def slopes_of(step):
        _, _, top_ref, e_ref, s_ref = held[step]
        fade = jnp.exp(top_ref[...] - log_total)
        for t in range(keys // TILE):
            at = pl.ds(t * TILE, TILE)
            p = e_ref[at, :] * fade
            d_scr[step % 2, at, :] = (p * (s_ref[at, :] - delta)).astype(jnp.bfloat16)
            p_scr[step % 2, at, :] = p.astype(jnp.bfloat16)

    def products(step):
        k, kv_ref, _, _, _ = held[step]
        b = source(pos_ref, k, blocks)
        slot = step % 2
        dk = scale * jnp.dot(d_scr[slot], qs[...], preferred_element_type=jnp.float32)
        dv = jnp.dot(p_scr[slot], gs[...], preferred_element_type=jnp.float32)
        for half, grad in enumerate((dk, dv)):
            at = pl.ds(half * width, width)
            for piece in range(trunk // TILE):
                kv_scr[slot, piece % 2, piece // 2, :, at] = grad[piece * TILE : (piece + 1) * TILE]
            tree_scr[lax.div(b, 2), lax.rem(b, 2), :, at] = grad[trunk:]
        keep_ref[b] = kv_scr[slot, mine]
        send_ref[b] = kv_scr[slot, 1 - mine].astype(jnp.bfloat16)
        tree = pl.ds(step * TILE, TILE)
        tree_k[tree, :] = kv_ref[trunk:, :width]
        tree_d[tree, :] = d_scr[slot, trunk:, :]
        part = dot_tn(kv_ref[:trunk, :width], d_scr[slot, :trunk, :])
        if step == blocks - 1:
            part += dot_tn(tree_k[...], tree_d[...])
        if step == 0:
            dq_scr[...] = part
        else:
            dq_scr[...] += part

    slopes_of(0)
    for step in range(blocks):
        if step + 1 < blocks:
            slopes_of(step + 1)
        products(step)
    for h in range(lanes // rows):
        piece = (scale * dq_scr[:, pl.ds(h * rows, rows)]).T
        q_scr[:, :, :, pl.ds(h * width, width)] = piece.reshape(groups // 2, 2, own, width)
    qkeep_ref[...] = q_scr[:, q_low]
    qsend_ref[...] = q_scr[:, 1 - q_low].astype(jnp.bfloat16)
    tkeep_ref[...] = tree_scr[:, tree_low]
    tsend_ref[...] = tree_scr[:, 1 - tree_low]


def grads_scratch(keys, lanes, width, nx, ny, own):
    bf16 = jnp.bfloat16
    return [
        pltpu.VMEM((2, keys, lanes), bf16),
        pltpu.VMEM((2, keys, lanes), bf16),
        pltpu.VMEM((nx * TILE, lanes), bf16),
        pltpu.VMEM((nx * TILE, width), bf16),
        pltpu.VMEM((2, 2, (keys - TILE) // (2 * own), own, 2 * width), jnp.float32),
        pltpu.VMEM((nx // 2, 2, own, 2 * width), jnp.float32),
        pltpu.VMEM((width, lanes), jnp.float32),
        pltpu.VMEM((ny // 2, 2, own, width * lanes // (ny * own)), jnp.float32),
    ]


def swap(x, axis):
    return lax.all_to_all(x, axis, 0, 0)


def spread(x, axis):
    return swap(jnp.broadcast_to(x[None], (lax.axis_size(axis),) + x.shape), axis)


def turn(x, axis, k):
    n = lax.axis_size(axis)
    return lax.ppermute(x, axis, [(i, (i + k) % n) for i in range(n)])


def meet(x, axis, bit):
    return lax.ppermute(x, axis, [(i, i ^ bit) for i in range(lax.axis_size(axis))])


def pick(x, which):
    return lax.dynamic_index_in_dim(x, which, 0, keepdims=False)


def per_device(queries, out_grad, branch_kv, trunk_kv, parent, prefix):
    bf16, f32 = jnp.bfloat16, jnp.float32
    width = trunk_kv.shape[1] // 2
    own = queries.shape[1]
    heads = queries.shape[2] // width
    nx, ny = lax.axis_size("x"), lax.axis_size("yh")
    x, yh, core = lax.axis_index("x"), lax.axis_index("yh"), lax.axis_index("c")
    span = trunk_kv.shape[0] * nx
    rows = own * ny
    lanes = rows * heads
    pos = jnp.stack([x, core, yh])

    shape = jax.ShapeDtypeStruct
    vmem = pl.BlockSpec(memory_space=pltpu.VMEM)
    smem = pl.BlockSpec(memory_space=pltpu.SMEM)
    anywhere = pl.BlockSpec(memory_space=pl.ANY)
    qg, kv = pl.pallas_call(
        pack_kernel,
        out_shape=(
            shape((ny, 2) + queries.shape[1:], bf16),
            shape((trunk_kv.shape[0] + own, 2 * width), bf16),
        ),
        in_specs=[anywhere] * 4,
        out_specs=(anywhere, vmem),
        scratch_shapes=[
            pltpu.VMEM((2,) + queries.shape[1:], bf16),
            pltpu.SemaphoreType.DMA((4,)),
            pltpu.SemaphoreType.DMA((ny, 2)),
        ],
        name="pack",
    )(queries, out_grad, trunk_kv, branch_kv)
    qg = swap(qg, "yh")
    kvs = [turn(kv, "x", k) for k in range(1, nx)]
    kvs = [jnp.concatenate([trunk_kv, branch_kv[0]], axis=0)] + kvs
    shifts = ((0, 1), (2, 3))

    lim, reach = pl.pallas_call(
        functools.partial(masks_kernel, nx, own, span),
        out_shape=(shape((1, lanes), jnp.int32), shape((nx * own, lanes), f32)),
        in_specs=[smem, vmem, vmem],
        out_specs=(vmem, vmem),
        scratch_shapes=[pltpu.VMEM((parent.shape[1], parent.shape[1]), f32)],
        compiler_params=pltpu.CompilerParams(vmem_limit_bytes=4 << 20),
        name="masks",
    )(pos, parent, prefix)
    keys = kv.shape[0]
    head = (pos, lim, reach)
    rest = [qg]
    held = []
    for half in range(2):
        count = len(shifts[half])
        outs = [
            shape((3 - half, lanes), f32),
            shape((count, lanes), f32),
            shape((count, keys, lanes), f32),
            shape((count, keys, lanes), f32),
        ]
        if half == 0:
            outs += [shape((lanes, width), bf16)] * 2
        stats, tops, e, s, *stacked = pl.pallas_call(
            functools.partial(stats_kernel, shifts[half], half == 1),
            out_shape=tuple(outs),
            in_specs=[smem] + [vmem] * (2 + len(rest) + count),
            out_specs=(vmem,) * len(outs),
            compiler_params=pltpu.CompilerParams(vmem_limit_bytes=6 << 20),
            name="stats",
        )(*head, *rest, *[kvs[k] for k in shifts[half]])
        held += [tops, e, s]
        if half == 0:
            qs, gs = stacked
            rest = [qs, gs, stats]
    stats = spread(stats, "yh")
    pieces = trunk_kv.shape[0] // (2 * own)
    q_keep, q_send, keep, send, t_keep, t_send = pl.pallas_call(
        functools.partial(grads_kernel, shifts),
        out_shape=(
            shape((ny // 2, own, heads * width), f32),
            shape((ny // 2, own, heads * width), bf16),
            shape((nx, pieces, own, 2 * width), f32),
            shape((nx, pieces, own, 2 * width), bf16),
            shape((nx // 2, own, 2 * width), f32),
            shape((nx // 2, own, 2 * width), f32),
        ),
        in_specs=[smem] + [vmem] * (9 + nx),
        out_specs=(vmem,) * 6,
        scratch_shapes=grads_scratch(keys, lanes, width, nx, ny, own),
        compiler_params=pltpu.CompilerParams(vmem_limit_bytes=12 << 20),
        name="grads",
    )(pos, stats, qs, gs, *held, *kvs)
    other = turn(send, "c", 1)
    trunk = (keep + other.astype(f32)).astype(bf16).reshape(nx * pieces, own, 2 * width)
    trunk = swap(trunk, ("x", "z", "yl"))
    high = lax.div(yh, 2)
    part = q_keep + meet(q_send, "yh", 1).astype(f32)
    query_grad = pick(part, high) + meet(pick(part, 1 - high).astype(bf16), "yh", 2).astype(f32)
    query_grad = query_grad.astype(bf16)
    high = lax.div(x, 2)
    part = t_keep + meet(t_send, "x", 1)
    branch = pick(part, high) + meet(pick(part, 1 - high), "x", 2)
    trunk = jnp.sum(trunk.astype(f32), axis=0)
    return (query_grad[None], branch[None], trunk)


def solution(mesh):
    fine = Mesh(mesh.devices.reshape(4, 4, 8, 2, 2), ("yh", "x") + SET)
    ctx = ("yh", "x")
    return jax.shard_map(
        per_device,
        mesh=fine,
        in_specs=(
            P(SET, ctx, None),
            P(SET, ctx, None),
            P(SET, ctx, None),
            P(ctx, None),
            P(SET, None),
            P(SET, None),
        ),
        out_specs=(P(SET, ctx, None), P(SET, ctx, None), P(ctx + SET, None)),
        check_vma=False,
    )
```

```python
import functools
import math

import jax
import jax.numpy as jnp
from jax import lax
from jax.experimental import pallas as pl
from jax.experimental.pallas import tpu as pltpu
from jax.sharding import Mesh, PartitionSpec as P


MASKED = -1e30
TILE = 16
STRIP = 8
SET = ("z", "yl", "c")


def dot_nt(left, right):
    return lax.dot_general(
        left, right, (((1,), (1,)), ((), ())), preferred_element_type=jnp.float32
    )


def dot_tn(left, right):
    return lax.dot_general(
        left, right, (((0,), (0,)), ((), ())), preferred_element_type=jnp.float32
    )


def stack_heads(src, which, dst):
    groups, _, own, _ = src.shape
    width = dst.shape[1]
    rows = groups * own
    for h in range(dst.shape[0] // rows):
        for y in range(groups):
            dst[pl.ds(h * rows + y * own, own), :] = src[y, which, :, pl.ds(h * width, width)]


def source(pos_ref, k, blocks):
    return lax.rem(pos_ref[0] + blocks - k, blocks)


def masks_kernel(nx, own, span, pos_ref, trees_ref, lim_ref, reach_ref, closed):
    count = trees_ref.shape[1]
    lanes = lim_ref.shape[1]
    x, yh = pos_ref[0], pos_ref[2]
    above = lax.broadcasted_iota(jnp.int32, (count, count), 0)
    below = lax.broadcasted_iota(jnp.int32, (count, count), 1)
    reach = jnp.where((trees_ref[0:1, :] == above) | (above == below), 1.0, 0.0).astype(jnp.bfloat16)
    for _ in range(max(count - 1, 1).bit_length()):
        pairs = jnp.dot(reach, reach, preferred_element_type=jnp.float32)
        reach = jnp.minimum(pairs, 1.0).astype(jnp.bfloat16)
    closed[...] = reach.astype(jnp.float32)
    rows = count // nx
    lane = lax.broadcasted_iota(jnp.int32, (count, lanes), 1)
    row = lax.rem(lax.div(lane, own), rows // own) * (nx * own) + x * own + lax.rem(lane, own)
    chosen = jnp.where(lax.broadcasted_iota(jnp.int32, (count, lanes), 0) == row, 1.0, 0.0)
    chosen = chosen.astype(jnp.bfloat16)
    mine = closed[pl.ds(pl.multiple_of(yh * nx * own, nx * own), nx * own), :]
    reach_ref[...] = jnp.dot(mine.astype(jnp.bfloat16), chosen, preferred_element_type=jnp.float32)
    prefix = trees_ref[1:2, :]
    part = lax.broadcasted_iota(jnp.int32, (TILE, count), 0)
    digits = jnp.where(part == 0, lax.div(prefix, 128), lax.rem(prefix, 128))
    digits = jnp.dot(
        digits.astype(jnp.float32).astype(jnp.bfloat16), chosen, preferred_element_type=jnp.float32
    )
    lim = (digits[0:1] * 128.0 + digits[1:2]).astype(jnp.int32)
    lim_ref[...] = lim - yh * span


def stats_kernel(shifts, last, pos_ref, lim_ref, reach_ref, *refs):
    count = len(shifts)
    if last:
        qs, gs, before_ref = refs[:3]
        kvs = refs[3 : 3 + count]
        after_ref, tops_ref, e_ref, s_ref = refs[3 + count :]
    else:
        qg_ref = refs[0]
        kvs = refs[1 : 1 + count]
        after_ref, tops_ref, e_ref, s_ref, qs, gs = refs[1 + count :]
        stack_heads(qg_ref, 0, qs)
        stack_heads(qg_ref, 1, gs)
    keys, wide = kvs[0].shape
    width = wide // 2
    lanes = qs.shape[0]
    scale = width ** (-0.5)
    trunk = keys - TILE
    power = scale * math.log2(math.e)
    ids = lax.broadcasted_iota(jnp.int32, (trunk, lanes), 0)
    if last:
        top, total, slope = (before_ref[i : i + 1, :] for i in range(3))
    else:
        top = jnp.full((1, lanes), MASKED, jnp.float32)
        total = jnp.zeros((1, lanes), jnp.float32)
        slope = jnp.zeros((1, lanes), jnp.float32)
    nows = []

    def score(i):
        b = source(pos_ref, shifts[i], 4)
        raw = dot_nt(kvs[i][:, :width], qs[...])
        near = jnp.where(ids < lim_ref[...] - b * trunk, raw[:trunk], MASKED)
        tree = jnp.where(
            reach_ref[pl.ds(pl.multiple_of(b * TILE, TILE), TILE), :] > 0.5, raw[trunk:], MASKED
        )
        e_ref[i, :trunk, :] = near
        e_ref[i, trunk:, :] = tree
        best = jnp.maximum(
            jnp.max(near, axis=0, keepdims=True), jnp.max(tree, axis=0, keepdims=True)
        )
        s_ref[i] = dot_nt(kvs[i][:, width:], gs[...])
        nows.append(jnp.maximum(nows[-1] if nows else top, best))
        tops_ref[pl.ds(i, 1), :] = nows[-1] * scale

    def weigh(i, total, slope):
        now = nows[i]
        fade = jnp.exp2(((nows[i - 1] if i else top) - now) * power)
        l = jnp.zeros((STRIP, lanes), jnp.float32)
        d = jnp.zeros((STRIP, lanes), jnp.float32)
        for t in range(keys // STRIP):
            at = pl.ds(t * STRIP, STRIP)
            p = jnp.exp2((e_ref[i, at, :] - now) * power)
            l = l + p
            d = d + p * s_ref[i, at, :]
            e_ref[i, at, :] = p
        return (
            total * fade + jnp.sum(l, axis=0, keepdims=True),
            slope * fade + jnp.sum(d, axis=0, keepdims=True),
        )

    for i in range(count):
        score(i)
    for i in range(count):
        total, slope = weigh(i, total, slope)
    top = nows[-1]
    if last:
        after_ref[0:1, :] = top * scale + jnp.log(total)
        after_ref[1:2, :] = slope / total
    else:
        after_ref[0:1, :] = top
        after_ref[1:2, :] = total
        after_ref[2:3, :] = slope


def grads_kernel(shifts, pos_ref, stats_ref, qs, gs, *refs):
    blocks = len(shifts[0]) + len(shifts[1])
    kvs = refs[6 : 6 + blocks]
    held = [
        (k, kvs[k], refs[3 * half].at[pl.ds(i, 1)], refs[3 * half + 1].at[i], refs[3 * half + 2].at[i])
        for half in range(2)
        for i, k in enumerate(shifts[half])
    ]
    qkeep_ref, qsend_ref, keep_ref, send_ref, tkeep_ref, tsend_ref = refs[6 + blocks : 12 + blocks]
    d_scr, p_scr, tree_d, tree_k, kv_scr, tree_scr, dq_scr, q_scr = refs[12 + blocks :]
    _, keys, lanes = d_scr.shape
    groups = stats_ref.shape[0]
    own = qkeep_ref.shape[1]
    rows = groups * own
    width = qs.shape[1]
    scale = width ** (-0.5)
    trunk = keys - TILE
    mine = pos_ref[1]
    q_low = lax.rem(pos_ref[2], 2)
    tree_low = lax.rem(pos_ref[0], 2)
    parts = [stats_ref[i, 0:1, :] for i in range(groups)]
    top = parts[0]
    for part in parts[1:]:
        top = jnp.maximum(top, part)
    total = jnp.zeros_like(top)
    for part in parts:
        total = total + jnp.exp(part - top)
    log_total = top + jnp.log(total)
    delta = jnp.zeros_like(top)
    for i in range(groups):
        delta = delta + jnp.exp(parts[i] - log_total) * stats_ref[i, 1:2, :]

    def slopes_of(step):
        _, _, top_ref, e_ref, s_ref = held[step]
        fade = jnp.exp(top_ref[...] - log_total)
        for t in range(keys // TILE):
            at = pl.ds(t * TILE, TILE)
            p = e_ref[at, :] * fade
            d_scr[step % 2, at, :] = (p * (s_ref[at, :] - delta)).astype(jnp.bfloat16)
            p_scr[step % 2, at, :] = p.astype(jnp.bfloat16)

    def products(step):
        k, kv_ref, _, _, _ = held[step]
        b = source(pos_ref, k, blocks)
        slot = step % 2
        dk = scale * jnp.dot(d_scr[slot], qs[...], preferred_element_type=jnp.float32)
        dv = jnp.dot(p_scr[slot], gs[...], preferred_element_type=jnp.float32)
        for half, grad in enumerate((dk, dv)):
            at = pl.ds(half * width, width)
            for piece in range(trunk // TILE):
                kv_scr[slot, piece % 2, piece // 2, :, at] = grad[piece * TILE : (piece + 1) * TILE]
            tree_scr[lax.div(b, 2), lax.rem(b, 2), :, at] = grad[trunk:]
        keep_ref[b] = kv_scr[slot, mine]
        send_ref[b] = kv_scr[slot, 1 - mine].astype(jnp.bfloat16)
        tree = pl.ds(step * TILE, TILE)
        tree_k[tree, :] = kv_ref[trunk:, :width]
        tree_d[tree, :] = d_scr[slot, trunk:, :]
        part = dot_tn(kv_ref[:trunk, :width], d_scr[slot, :trunk, :])
        if step == blocks - 1:
            part += dot_tn(tree_k[...], tree_d[...])
        if step == 0:
            dq_scr[...] = part
        else:
            dq_scr[...] += part

    slopes_of(0)
    for step in range(blocks):
        if step + 1 < blocks:
            slopes_of(step + 1)
        products(step)
    for h in range(lanes // rows):
        piece = (scale * dq_scr[:, pl.ds(h * rows, rows)]).T
        q_scr[:, :, :, pl.ds(h * width, width)] = piece.reshape(groups // 2, 2, own, width)
    qkeep_ref[...] = q_scr[:, q_low]
    qsend_ref[...] = q_scr[:, 1 - q_low].astype(jnp.bfloat16)
    tkeep_ref[...] = tree_scr[:, tree_low]
    tsend_ref[...] = tree_scr[:, 1 - tree_low]


def grads_scratch(keys, lanes, width, nx, ny, own):
    bf16 = jnp.bfloat16
    return [
        pltpu.VMEM((2, keys, lanes), bf16),
        pltpu.VMEM((2, keys, lanes), bf16),
        pltpu.VMEM((nx * TILE, lanes), bf16),
        pltpu.VMEM((nx * TILE, width), bf16),
        pltpu.VMEM((2, 2, (keys - TILE) // (2 * own), own, 2 * width), jnp.float32),
        pltpu.VMEM((nx // 2, 2, own, 2 * width), jnp.float32),
        pltpu.VMEM((width, lanes), jnp.float32),
        pltpu.VMEM((ny // 2, 2, own, width * lanes // (ny * own)), jnp.float32),
    ]


def swap(x, axis):
    return lax.all_to_all(x, axis, 0, 0)


def spread(x, axis):
    return swap(jnp.broadcast_to(x[None], (lax.axis_size(axis),) + x.shape), axis)


def turn(x, axis, k):
    n = lax.axis_size(axis)
    return lax.ppermute(x, axis, [(i, (i + k) % n) for i in range(n)])


def meet(x, axis, bit):
    return lax.ppermute(x, axis, [(i, i ^ bit) for i in range(lax.axis_size(axis))])


def pick(x, which):
    return lax.dynamic_index_in_dim(x, which, 0, keepdims=False)


def per_device(queries, out_grad, branch_kv, trunk_kv, parent, prefix):
    bf16, f32 = jnp.bfloat16, jnp.float32
    width = trunk_kv.shape[1] // 2
    own = queries.shape[1]
    heads = queries.shape[2] // width
    nx, ny = lax.axis_size("x"), lax.axis_size("yh")
    x, yh, core = lax.axis_index("x"), lax.axis_index("yh"), lax.axis_index("c")
    span = trunk_kv.shape[0] * nx
    rows = own * ny
    lanes = rows * heads
    pos = jnp.stack([x, core, yh])

    shape = jax.ShapeDtypeStruct
    vmem = pl.BlockSpec(memory_space=pltpu.VMEM)
    smem = pl.BlockSpec(memory_space=pltpu.SMEM)
    qg = spread(jnp.stack([queries[0], out_grad[0]]), "yh")
    kv = jnp.concatenate([trunk_kv, branch_kv[0]], axis=0)
    kvs = [kv] + [None] * (nx - 1)
    for k in range(1, nx):
        kvs[k] = turn(kv, "x", k)
    shifts = ((0, 1), (2, 3))

    lim, reach = pl.pallas_call(
        functools.partial(masks_kernel, nx, own, span),
        out_shape=(shape((1, lanes), jnp.int32), shape((nx * own, lanes), f32)),
        in_specs=[smem, vmem],
        out_specs=(vmem, vmem),
        scratch_shapes=[pltpu.VMEM((parent.shape[1], parent.shape[1]), f32)],
        compiler_params=pltpu.CompilerParams(vmem_limit_bytes=4 << 20),
        name="masks",
    )(pos, jnp.concatenate([parent, prefix], axis=0))
    keys = kv.shape[0]
    head = (pos, lim, reach)
    rest = [qg]
    held = []
    for half in range(2):
        count = len(shifts[half])
        outs = [
            shape((3 - half, lanes), f32),
            shape((count, lanes), f32),
            shape((count, keys, lanes), f32),
            shape((count, keys, lanes), f32),
        ]
        if half == 0:
            outs += [shape((lanes, width), bf16)] * 2
        stats, tops, e, s, *stacked = pl.pallas_call(
            functools.partial(stats_kernel, shifts[half], half == 1),
            out_shape=tuple(outs),
            in_specs=[smem] + [vmem] * (2 + len(rest) + count),
            out_specs=(vmem,) * len(outs),
            compiler_params=pltpu.CompilerParams(vmem_limit_bytes=6 << 20),
            name="stats",
        )(*head, *rest, *[kvs[k] for k in shifts[half]])
        held += [tops, e, s]
        if half == 0:
            qs, gs = stacked
            rest = [qs, gs, stats]
    stats = spread(stats, "yh")
    pieces = trunk_kv.shape[0] // (2 * own)
    q_keep, q_send, keep, send, t_keep, t_send = pl.pallas_call(
        functools.partial(grads_kernel, shifts),
        out_shape=(
            shape((ny // 2, own, heads * width), f32),
            shape((ny // 2, own, heads * width), bf16),
            shape((nx, pieces, own, 2 * width), f32),
            shape((nx, pieces, own, 2 * width), bf16),
            shape((nx // 2, own, 2 * width), f32),
            shape((nx // 2, own, 2 * width), f32),
        ),
        in_specs=[smem] + [vmem] * (9 + nx),
        out_specs=(vmem,) * 6,
        scratch_shapes=grads_scratch(keys, lanes, width, nx, ny, own),
        compiler_params=pltpu.CompilerParams(vmem_limit_bytes=12 << 20),
        name="grads",
    )(pos, stats, qs, gs, *held, *kvs)
    other = turn(send, "c", 1)
    trunk = (keep + other.astype(f32)).astype(bf16).reshape(nx * pieces, own, 2 * width)
    trunk = swap(trunk, ("x", "z", "yl"))
    high = lax.div(yh, 2)
    part = q_keep + meet(q_send, "yh", 1).astype(f32)
    rest = meet(pick(part, 1 - high).astype(bf16), "yh", 2)
    query_grad = (pick(part, high) + rest.astype(f32)).astype(bf16)
    high = lax.div(x, 2)
    part = t_keep + meet(t_send, "x", 1)
    branch = pick(part, high) + meet(pick(part, 1 - high), "x", 2)
    trunk = jnp.sum(trunk.astype(f32), axis=0)
    return (query_grad[None], branch[None], trunk)


def solution(mesh):
    fine = Mesh(mesh.devices.reshape(4, 4, 8, 2, 2), ("yh", "x") + SET)
    ctx = ("yh", "x")
    return jax.shard_map(
        per_device,
        mesh=fine,
        in_specs=(
            P(SET, ctx, None),
            P(SET, ctx, None),
            P(SET, ctx, None),
            P(ctx, None),
            P(SET, None),
            P(SET, None),
        ),
        out_specs=(P(SET, ctx, None), P(SET, ctx, None), P(ctx + SET, None)),
        check_vma=False,
    )
```

```python
import functools
import math

import jax
import jax.numpy as jnp
from jax import lax
from jax.experimental import pallas as pl
from jax.experimental.pallas import tpu as pltpu
from jax.sharding import Mesh, PartitionSpec as P


MASKED = -1e30
TILE = 16
STRIP = 8
SET = ("z", "yl", "c")


def dot_nt(left, right):
    return lax.dot_general(
        left, right, (((1,), (1,)), ((), ())), preferred_element_type=jnp.float32
    )


def dot_tn(left, right):
    return lax.dot_general(
        left, right, (((0,), (0,)), ((), ())), preferred_element_type=jnp.float32
    )


def stack_heads(src, which, dst):
    groups, _, own, _ = src.shape
    width = dst.shape[1]
    rows = groups * own
    for h in range(dst.shape[0] // rows):
        for y in range(groups):
            dst[pl.ds(h * rows + y * own, own), :] = src[y, which, :, pl.ds(h * width, width)]


def source(pos_ref, k, blocks):
    return lax.rem(pos_ref[0] + blocks - k, blocks)


def masks_kernel(nx, own, span, pos_ref, trees_ref, lim_ref, reach_ref, closed):
    count = trees_ref.shape[1]
    lanes = lim_ref.shape[1]
    x, yh = pos_ref[0], pos_ref[2]
    above = lax.broadcasted_iota(jnp.int32, (count, count), 0)
    below = lax.broadcasted_iota(jnp.int32, (count, count), 1)
    reach = jnp.where((trees_ref[0:1, :] == above) | (above == below), 1.0, 0.0).astype(jnp.bfloat16)
    for _ in range(max(count - 1, 1).bit_length()):
        pairs = jnp.dot(reach, reach, preferred_element_type=jnp.float32)
        reach = jnp.minimum(pairs, 1.0).astype(jnp.bfloat16)
    closed[...] = reach.astype(jnp.float32)
    rows = count // nx
    lane = lax.broadcasted_iota(jnp.int32, (count, lanes), 1)
    row = lax.rem(lax.div(lane, own), rows // own) * (nx * own) + x * own + lax.rem(lane, own)
    chosen = jnp.where(lax.broadcasted_iota(jnp.int32, (count, lanes), 0) == row, 1.0, 0.0)
    chosen = chosen.astype(jnp.bfloat16)
    mine = closed[pl.ds(pl.multiple_of(yh * nx * own, nx * own), nx * own), :]
    reach_ref[...] = jnp.dot(mine.astype(jnp.bfloat16), chosen, preferred_element_type=jnp.float32)
    prefix = trees_ref[1:2, :]
    part = lax.broadcasted_iota(jnp.int32, (TILE, count), 0)
    digits = jnp.where(part == 0, lax.div(prefix, 128), lax.rem(prefix, 128))
    digits = jnp.dot(
        digits.astype(jnp.float32).astype(jnp.bfloat16), chosen, preferred_element_type=jnp.float32
    )
    lim = (digits[0:1] * 128.0 + digits[1:2]).astype(jnp.int32)
    lim_ref[...] = lim - yh * span


def stats_kernel(shifts, first, last, pos_ref, lim_ref, reach_ref, *refs):
    count = len(shifts)
    if not first:
        qs, gs, before_ref = refs[:3]
        kvs = refs[3 : 3 + count]
        after_ref, tops_ref, e_ref, s_ref = refs[3 + count :]
    else:
        qg_ref = refs[0]
        kvs = refs[1 : 1 + count]
        after_ref, tops_ref, e_ref, s_ref, qs, gs = refs[1 + count :]
        stack_heads(qg_ref, 0, qs)
        stack_heads(qg_ref, 1, gs)
    keys, wide = kvs[0].shape
    width = wide // 2
    lanes = qs.shape[0]
    scale = width ** (-0.5)
    trunk = keys - TILE
    power = scale * math.log2(math.e)
    ids = lax.broadcasted_iota(jnp.int32, (trunk, lanes), 0)
    if not first:
        top, total, slope = (before_ref[i : i + 1, :] for i in range(3))
    else:
        top = jnp.full((1, lanes), MASKED, jnp.float32)
        total = jnp.zeros((1, lanes), jnp.float32)
        slope = jnp.zeros((1, lanes), jnp.float32)
    nows = []

    def score(i):
        b = source(pos_ref, shifts[i], 4)
        raw = dot_nt(kvs[i][:, :width], qs[...])
        near = jnp.where(ids < lim_ref[...] - b * trunk, raw[:trunk], MASKED)
        tree = jnp.where(
            reach_ref[pl.ds(pl.multiple_of(b * TILE, TILE), TILE), :] > 0.5, raw[trunk:], MASKED
        )
        e_ref[i, :trunk, :] = near
        e_ref[i, trunk:, :] = tree
        best = jnp.maximum(
            jnp.max(near, axis=0, keepdims=True), jnp.max(tree, axis=0, keepdims=True)
        )
        s_ref[i] = dot_nt(kvs[i][:, width:], gs[...])
        nows.append(jnp.maximum(nows[-1] if nows else top, best))
        tops_ref[pl.ds(i, 1), :] = nows[-1] * scale

    def weigh(i, total, slope):
        now = nows[i]
        fade = jnp.exp2(((nows[i - 1] if i else top) - now) * power)
        l = jnp.zeros((STRIP, lanes), jnp.float32)
        d = jnp.zeros((STRIP, lanes), jnp.float32)
        for t in range(keys // STRIP):
            at = pl.ds(t * STRIP, STRIP)
            p = jnp.exp2((e_ref[i, at, :] - now) * power)
            l = l + p
            d = d + p * s_ref[i, at, :]
            e_ref[i, at, :] = p
        return (
            total * fade + jnp.sum(l, axis=0, keepdims=True),
            slope * fade + jnp.sum(d, axis=0, keepdims=True),
        )

    for i in range(count):
        score(i)
    for i in range(count):
        total, slope = weigh(i, total, slope)
    top = nows[-1]
    if last:
        after_ref[0:1, :] = top * scale + jnp.log(total)
        after_ref[1:2, :] = slope / total
    else:
        after_ref[0:1, :] = top
        after_ref[1:2, :] = total
        after_ref[2:3, :] = slope


def grads_kernel(shifts, pos_ref, stats_ref, qs, gs, *refs):
    calls = len(shifts)
    blocks = sum(map(len, shifts))
    kvs = refs[3 * calls : 3 * calls + blocks]
    refs = refs[:3 * calls] + refs[3 * calls + blocks :]
    held = [
        (k, kvs[k], refs[3 * half].at[pl.ds(i, 1)], refs[3 * half + 1].at[i], refs[3 * half + 2].at[i])
        for half in range(calls)
        for i, k in enumerate(shifts[half])
    ]
    qkeep_ref, qsend_ref, keep_ref, send_ref, tkeep_ref, tsend_ref = refs[3 * calls :][:6]
    d_scr, p_scr, tree_d, tree_k, kv_scr, tree_scr, dq_scr, q_scr = refs[3 * calls + 6 :]
    _, keys, lanes = d_scr.shape
    groups = stats_ref.shape[0]
    own = qkeep_ref.shape[1]
    rows = groups * own
    width = qs.shape[1]
    scale = width ** (-0.5)
    trunk = keys - TILE
    mine = pos_ref[1]
    q_low = lax.rem(pos_ref[2], 2)
    tree_low = lax.rem(pos_ref[0], 2)
    parts = [stats_ref[i, 0:1, :] for i in range(groups)]
    top = parts[0]
    for part in parts[1:]:
        top = jnp.maximum(top, part)
    total = jnp.zeros_like(top)
    for part in parts:
        total = total + jnp.exp(part - top)
    log_total = top + jnp.log(total)
    delta = jnp.zeros_like(top)
    for i in range(groups):
        delta = delta + jnp.exp(parts[i] - log_total) * stats_ref[i, 1:2, :]

    def slopes_of(step):
        _, _, top_ref, e_ref, s_ref = held[step]
        fade = jnp.exp(top_ref[...] - log_total)
        for t in range(keys // TILE):
            at = pl.ds(t * TILE, TILE)
            p = e_ref[at, :] * fade
            d_scr[step % 2, at, :] = (p * (s_ref[at, :] - delta)).astype(jnp.bfloat16)
            p_scr[step % 2, at, :] = p.astype(jnp.bfloat16)

    def products(step):
        k, kv_ref, _, _, _ = held[step]
        b = source(pos_ref, k, blocks)
        slot = step % 2
        dk = scale * jnp.dot(d_scr[slot], qs[...], preferred_element_type=jnp.float32)
        dv = jnp.dot(p_scr[slot], gs[...], preferred_element_type=jnp.float32)
        for half, grad in enumerate((dk, dv)):
            at = pl.ds(half * width, width)
            for piece in range(trunk // TILE):
                kv_scr[slot, piece % 2, piece // 2, :, at] = grad[piece * TILE : (piece + 1) * TILE]
            tree_scr[lax.div(b, 2), lax.rem(b, 2), :, at] = grad[trunk:]
        keep_ref[b] = kv_scr[slot, mine]
        send_ref[b] = kv_scr[slot, 1 - mine].astype(jnp.bfloat16)
        tree = pl.ds(step * TILE, TILE)
        tree_k[tree, :] = kv_ref[trunk:, :width]
        tree_d[tree, :] = d_scr[slot, trunk:, :]
        part = dot_tn(kv_ref[:trunk, :width], d_scr[slot, :trunk, :])
        if step == blocks - 1:
            part += dot_tn(tree_k[...], tree_d[...])
        if step == 0:
            dq_scr[...] = part
        else:
            dq_scr[...] += part

    slopes_of(0)
    for step in range(blocks):
        if step + 1 < blocks:
            slopes_of(step + 1)
        products(step)
    for h in range(lanes // rows):
        piece = (scale * dq_scr[:, pl.ds(h * rows, rows)]).T
        q_scr[:, :, :, pl.ds(h * width, width)] = piece.reshape(groups // 2, 2, own, width)
    qkeep_ref[...] = q_scr[:, q_low]
    qsend_ref[...] = q_scr[:, 1 - q_low].astype(jnp.bfloat16)
    tkeep_ref[...] = tree_scr[:, tree_low]
    tsend_ref[...] = tree_scr[:, 1 - tree_low]


def grads_scratch(keys, lanes, width, nx, ny, own):
    bf16 = jnp.bfloat16
    return [
        pltpu.VMEM((2, keys, lanes), bf16),
        pltpu.VMEM((2, keys, lanes), bf16),
        pltpu.VMEM((nx * TILE, lanes), bf16),
        pltpu.VMEM((nx * TILE, width), bf16),
        pltpu.VMEM((2, 2, (keys - TILE) // (2 * own), own, 2 * width), jnp.float32),
        pltpu.VMEM((nx // 2, 2, own, 2 * width), jnp.float32),
        pltpu.VMEM((width, lanes), jnp.float32),
        pltpu.VMEM((ny // 2, 2, own, width * lanes // (ny * own)), jnp.float32),
    ]


def swap(x, axis):
    return lax.all_to_all(x, axis, 0, 0)


def spread(x, axis):
    return swap(jnp.broadcast_to(x[None], (lax.axis_size(axis),) + x.shape), axis)


def turn(x, axis, k):
    n = lax.axis_size(axis)
    return lax.ppermute(x, axis, [(i, (i + k) % n) for i in range(n)])


def meet(x, axis, bit):
    return lax.ppermute(x, axis, [(i, i ^ bit) for i in range(lax.axis_size(axis))])


def pick(x, which):
    return lax.dynamic_index_in_dim(x, which, 0, keepdims=False)


def per_device(queries, out_grad, branch_kv, trunk_kv, parent, prefix):
    bf16, f32 = jnp.bfloat16, jnp.float32
    width = trunk_kv.shape[1] // 2
    own = queries.shape[1]
    heads = queries.shape[2] // width
    nx, ny = lax.axis_size("x"), lax.axis_size("yh")
    x, yh, core = lax.axis_index("x"), lax.axis_index("yh"), lax.axis_index("c")
    span = trunk_kv.shape[0] * nx
    rows = own * ny
    lanes = rows * heads
    pos = jnp.stack([x, core, yh])

    shape = jax.ShapeDtypeStruct
    vmem = pl.BlockSpec(memory_space=pltpu.VMEM)
    smem = pl.BlockSpec(memory_space=pltpu.SMEM)
    qg = spread(jnp.stack([queries[0], out_grad[0]]), "yh")
    kv = jnp.concatenate([trunk_kv, branch_kv[0]], axis=0)
    kvs = [kv] + [None] * (nx - 1)
    for k in range(1, nx):
        kvs[k] = turn(kv, "x", k)
    shifts = ((0, 2), (1,), (3,))

    lim, reach = pl.pallas_call(
        functools.partial(masks_kernel, nx, own, span),
        out_shape=(shape((1, lanes), jnp.int32), shape((nx * own, lanes), f32)),
        in_specs=[smem, vmem],
        out_specs=(vmem, vmem),
        scratch_shapes=[pltpu.VMEM((parent.shape[1], parent.shape[1]), f32)],
        compiler_params=pltpu.CompilerParams(vmem_limit_bytes=4 << 20),
        name="masks",
    )(pos, jnp.concatenate([parent, prefix], axis=0))
    keys = kv.shape[0]
    head = (pos, lim, reach)
    rest = [qg]
    held = []
    for half in range(len(shifts)):
        first, last = half == 0, half == len(shifts) - 1
        count = len(shifts[half])
        outs = [
            shape((2 if last else 3, lanes), f32),
            shape((count, lanes), f32),
            shape((count, keys, lanes), f32),
            shape((count, keys, lanes), f32),
        ]
        if first:
            outs += [shape((lanes, width), bf16)] * 2
        stats, tops, e, s, *stacked = pl.pallas_call(
            functools.partial(stats_kernel, shifts[half], first, last),
            out_shape=tuple(outs),
            in_specs=[smem] + [vmem] * (2 + len(rest) + count),
            out_specs=(vmem,) * len(outs),
            compiler_params=pltpu.CompilerParams(vmem_limit_bytes=6 << 20),
            name="stats",
        )(*head, *rest, *[kvs[k] for k in shifts[half]])
        held += [tops, e, s]
        if first:
            qs, gs = stacked
        rest = [qs, gs, stats]
    stats = spread(stats, "yh")
    pieces = trunk_kv.shape[0] // (2 * own)
    q_keep, q_send, keep, send, t_keep, t_send = pl.pallas_call(
        functools.partial(grads_kernel, shifts),
        out_shape=(
            shape((ny // 2, own, heads * width), f32),
            shape((ny // 2, own, heads * width), bf16),
            shape((nx, pieces, own, 2 * width), f32),
            shape((nx, pieces, own, 2 * width), bf16),
            shape((nx // 2, own, 2 * width), f32),
            shape((nx // 2, own, 2 * width), f32),
        ),
        in_specs=[smem] + [vmem] * (3 + len(held) + nx),
        out_specs=(vmem,) * 6,
        scratch_shapes=grads_scratch(keys, lanes, width, nx, ny, own),
        compiler_params=pltpu.CompilerParams(vmem_limit_bytes=12 << 20),
        name="grads",
    )(pos, stats, qs, gs, *held, *kvs)
    other = turn(send, "c", 1)
    trunk = (keep + other.astype(f32)).astype(bf16).reshape(nx * pieces, own, 2 * width)
    trunk = swap(trunk, ("x", "z", "yl"))
    high = lax.div(yh, 2)
    part = q_keep + meet(q_send, "yh", 1).astype(f32)
    rest = meet(pick(part, 1 - high).astype(bf16), "yh", 2)
    query_grad = (pick(part, high) + rest.astype(f32)).astype(bf16)
    high = lax.div(x, 2)
    part = t_keep + meet(t_send, "x", 1)
    branch = pick(part, high) + meet(pick(part, 1 - high), "x", 2)
    trunk = jnp.sum(trunk.astype(f32), axis=0)
    return (query_grad[None], branch[None], trunk)


def solution(mesh):
    fine = Mesh(mesh.devices.reshape(4, 4, 8, 2, 2), ("yh", "x") + SET)
    ctx = ("yh", "x")
    return jax.shard_map(
        per_device,
        mesh=fine,
        in_specs=(
            P(SET, ctx, None),
            P(SET, ctx, None),
            P(SET, ctx, None),
            P(ctx, None),
            P(SET, None),
            P(SET, None),
        ),
        out_specs=(P(SET, ctx, None), P(SET, ctx, None), P(ctx + SET, None)),
        check_vma=False,
    )
```
